256 devices in a mesh: ctx: 16 (over y, z_lo, core), fsdp: 16 (over x, z_hi).
Axes of the slice: x: 4, y: 4, z: 8 (z_hi: 4, z_lo: 2; z = z_hi * 2 + z_lo), core: 2. Of those that a mesh axis runs over, the one named last changes fastest.
Arguments:
- queries: bfloat16 [16, 4096, 2048], P('fsdp', 'ctx'), may hold values from -6 to 6
- keys: bfloat16 [16, 4096, 2048], P('fsdp', 'ctx'), may hold values from -6 to 6
- values: bfloat16 [16, 4096, 2048], P('fsdp', 'ctx'), may hold values from -6 to 6
- out_weight: bfloat16 [2048, 2048], P('fsdp'), may hold values from -0.125 to 0.125
- out_grad: bfloat16 [16, 4096, 2048], P('fsdp', 'ctx'), may hold values from -6 to 6
Outputs:
- grad_queries: bfloat16 [16, 4096, 2048], P('fsdp', 'ctx')
- grad_keys: bfloat16 [16, 4096, 2048], P('fsdp', 'ctx')
- grad_values: bfloat16 [16, 4096, 2048], P('fsdp', 'ctx')
- grad_weight: float32 [2048, 2048], P('fsdp')
The draws below stay inside these ranges and needn't reach their ends.
All inputs are finite; a program needn't handle non-finite values.
Results may differ from the reference program's by a relative error of at most 0.008.
Values may be sent and summed in bfloat16 or wider, within the bound.
No kernel may reach another device: no remote copies, remote signals or barrier semaphores. Data moves between devices by JAX's collectives and lax.ppermute only.
A program may use at most 128 MiB of HBM per device.

```python
import jax
import jax.numpy as jnp
from jax import lax

D = 2048
HEADS = 16
HEAD = 128
BLOCK = 256
TOK_DEV = 256
SEQS = 16
LENGTH = 4096
N_CTX = 16


def block_levels(rng, dims, shards, smallest, largest):
    level, own = 1.0, jax.random.fold_in(rng, 6)
    for axis_at, blocks in shards:
        steps = jnp.exp(jax.random.uniform(jax.random.fold_in(own, axis_at), (blocks,), jnp.float32, smallest / len(shards), largest / len(shards)))
        level = level * jnp.repeat(steps, dims[axis_at] // blocks).reshape([-1 if axis == axis_at else 1 for axis in range(len(dims))])
    return level


def noise(key, shape, spread, reach, split=(), held_as=jnp.bfloat16):
    level = block_levels(key, shape, split, -0.22, 0.18) if split else 1.0
    array = jax.random.normal(key, shape, jnp.float32) * spread * level
    return jnp.minimum(jnp.maximum(array, -reach), reach).astype(held_as)


def setup_inputs(seed: int = 0) -> dict:
    arg_keys = jax.random.split(jax.random.key(seed), 6)
    queries = noise(arg_keys[0], (SEQS, LENGTH, HEADS * HEAD), 1.0, 6.0, ((0, 16), (1, 16)))
    keys = noise(arg_keys[1], (SEQS, LENGTH, HEADS * HEAD), 1.0, 6.0, ((0, 16), (1, 16)))
    values = noise(arg_keys[2], (SEQS, LENGTH, HEADS * HEAD), 1.0, 6.0, ((0, 16), (1, 16)))
    out_weight = noise(arg_keys[3], (HEADS * HEAD, D), D ** -0.5, 0.125, ((0, 16),))
    out_grad = noise(arg_keys[4], (SEQS, LENGTH, D), 1.0, 6.0, ((0, 16), (1, 16)))
    return {"queries": queries, "keys": keys, "values": values, "out_weight": out_weight, "out_grad": out_grad}


HIGHEST = lax.Precision.HIGHEST


def rounded(array_in):
    return lax.optimization_barrier(array_in.astype(jnp.bfloat16)).astype(jnp.float32)


def sequence_terms(packed):
    queries_seq, keys_seq, values_seq, grad_seq = packed
    blocks_count = queries_seq.shape[0] // BLOCK
    layout = (blocks_count, BLOCK, HEADS, HEAD)
    query_blocks = queries_seq.reshape(layout).astype(jnp.float32)
    key_blocks = keys_seq.reshape(layout).astype(jnp.float32)
    value_blocks = values_seq.reshape(layout).astype(jnp.float32)
    grad_blocks = grad_seq.reshape(layout).astype(jnp.float32)
    key_states = jnp.einsum("bthd,bthe->bhde", key_blocks, value_blocks, precision=HIGHEST)
    grad_states = jnp.einsum("bthd,bthe->bhde", query_blocks, grad_blocks, precision=HIGHEST)
    prior_states = jnp.cumsum(key_states, 0) - key_states
    later_states = jnp.sum(grad_states, 0)[None] - jnp.cumsum(grad_states, 0)
    factor = (HEAD * LENGTH) ** -0.5
    positions = jnp.arange(BLOCK)
    causal = positions[:, None] >= positions[None, :]
    scores = rounded(jnp.where(causal, jnp.einsum("bthd,bshd->bhts", query_blocks, key_blocks, precision=HIGHEST), 0.0))
    reverse = rounded(jnp.where(causal, jnp.einsum("bthe,bshe->bhts", grad_blocks, value_blocks, precision=HIGHEST), 0.0))
    attended = factor * (jnp.einsum("bthd,bhde->bthe", query_blocks, prior_states, precision=HIGHEST)
                         + jnp.einsum("bhts,bshe->bthe", scores, value_blocks, precision=HIGHEST))
    grad_queries = factor * (jnp.einsum("bthe,bhde->bthd", grad_blocks, prior_states, precision=HIGHEST)
                             + jnp.einsum("bhts,bshd->bthd", reverse, key_blocks, precision=HIGHEST))
    grad_keys = factor * (jnp.einsum("bshe,bhde->bshd", value_blocks, later_states, precision=HIGHEST)
                          + jnp.einsum("bhts,bthd->bshd", reverse, query_blocks, precision=HIGHEST))
    grad_values = factor * (jnp.einsum("bshd,bhde->bshe", key_blocks, later_states, precision=HIGHEST)
                            + jnp.einsum("bhts,bthe->bshe", scores, grad_blocks, precision=HIGHEST))
    inner_width = HEADS * HEAD
    return (attended.reshape(-1, inner_width).astype(jnp.bfloat16),
            grad_queries.reshape(-1, inner_width).astype(jnp.bfloat16),
            grad_keys.reshape(-1, inner_width).astype(jnp.bfloat16),
            grad_values.reshape(-1, inner_width).astype(jnp.bfloat16))


def reference(queries, keys, values, out_weight, out_grad):
    def project(grad_seq):
        return jnp.dot(grad_seq, out_weight.T, preferred_element_type=jnp.float32).astype(jnp.bfloat16)

    grad_attn = lax.map(project, out_grad)
    attended, grad_queries, grad_keys, grad_values = lax.map(sequence_terms, (queries, keys, values, grad_attn))
    slab_count = SEQS * N_CTX
    attended_slabs = attended.reshape(slab_count, TOK_DEV, HEADS * HEAD)
    grad_slabs = out_grad.reshape(slab_count, TOK_DEV, D)

    def accumulate(running, slab_pair):
        slab_term = jnp.dot(slab_pair[0].T, slab_pair[1], preferred_element_type=jnp.float32)
        return running + slab_term, None

    summed, unused = lax.scan(accumulate, jnp.zeros((HEADS * HEAD, D), jnp.float32), (attended_slabs, grad_slabs))
    grad_weight = summed * (SEQS * LENGTH) ** -0.5
    return grad_queries, grad_keys, grad_values, grad_weight
```

```python
import functools

import jax
import jax.numpy as jnp
from jax import lax
from jax.experimental import pallas as pl
from jax.experimental.pallas import tpu as pltpu
from jax.sharding import PartitionSpec as P

HEADS = 16
HEAD = 128
F32 = jnp.float32
BF16 = jnp.bfloat16


def dot(a, b, da, db):
    return lax.dot_general(a, b, (((da,), (db,)), ((), ())), preferred_element_type=F32)


def from_core(v):
    return lax.ppermute(v, "ctx", [(i, i ^ 1) for i in range(16)])


def from_zl(v):
    return lax.ppermute(v, "ctx", [(i, i ^ 2) for i in range(16)])


def from_y(v, k):
    return lax.ppermute(v, "ctx", [((i + 4 * k) % 16, i) for i in range(16)])


def from_x(v, k):
    return lax.ppermute(v, "fsdp", [((i + 4 * k) % 16, i) for i in range(16)])


def from_zh(v, k):
    return lax.ppermute(v, "fsdp", [(i // 4 * 4 + (i + k) % 4, i) for i in range(16)])


def call(body, out, *args, grid=None, in_specs=None, out_specs=None, scratch=(), flops=0, name=None):
    size = sum(a.size * a.dtype.itemsize for a in args)
    outs = out if isinstance(out, (tuple, list)) else [out]
    size += sum(o.size * jnp.dtype(o.dtype).itemsize for o in outs)
    kwargs = {}
    if grid is not None:
        kwargs = dict(grid=grid, in_specs=in_specs, out_specs=out_specs)
    else:
        full = pl.BlockSpec(memory_space=pltpu.VMEM)
        small = pl.BlockSpec(memory_space=pltpu.SMEM)
        kwargs = dict(
            in_specs=[small if a.dtype == jnp.int32 else full for a in args],
            out_specs=jax.tree.map(lambda o: full, out),
        )
    return pl.pallas_call(
        body,
        out_shape=out,
        scratch_shapes=scratch,
        cost_estimate=pl.CostEstimate(flops=flops, bytes_accessed=size, transcendentals=0),
        name=name,
        **kwargs,
    )(*args)


def shape(dims, dtype=BF16):
    return jax.ShapeDtypeStruct(dims, dtype)


PER = 4


def head_slices():
    return [(h, slice(h * HEAD, (h + 1) * HEAD)) for h in range(PER)]


def rows_spec(tokens):
    return pl.BlockSpec((tokens, PER * HEAD), lambda i: (0, i))


STATE_SPEC = pl.BlockSpec((PER, HEAD, HEAD), lambda i: (i, 0, 0))


def states_body(a_ref, b_ref, o_ref):
    for h, s in head_slices():
        o_ref[h] = dot(a_ref[:, s], b_ref[:, s], 0, 0).astype(BF16)


def scan_body(reverse, i_ref, o_ref):
    count = i_ref.shape[0]
    total = jnp.zeros(i_ref.shape[1:], F32)
    for n in range(count):
        at = count - 1 - n if reverse else n
        o_ref[at] = total.astype(BF16)
        total = total + i_ref[at].astype(F32)


def causal(tokens):
    return lax.broadcasted_iota(jnp.int32, (tokens, tokens), 0) >= lax.broadcasted_iota(
        jnp.int32, (tokens, tokens), 1
    )


def attended_body(factor, q_ref, k_ref, v_ref, p_ref, o_ref):
    keep = causal(q_ref.shape[0])
    for h, s in head_slices():
        q = q_ref[:, s]
        scores = jnp.where(keep, dot(q, k_ref[:, s], 1, 1), 0.0).astype(BF16)
        o_ref[s, :] = (factor * (dot(p_ref[h], q, 0, 1) + dot(v_ref[:, s], scores, 0, 1))).astype(BF16)


def grad_queries_body(factor, g_ref, k_ref, v_ref, p_ref, o_ref):
    keep = causal(g_ref.shape[0])
    for h, s in head_slices():
        g = g_ref[:, s]
        reverse = jnp.where(keep, dot(g, v_ref[:, s], 1, 1), 0.0).astype(BF16)
        o_ref[:, s] = (factor * (dot(g, p_ref[h], 1, 1) + dot(reverse, k_ref[:, s], 1, 0))).astype(BF16)


def grad_keys_values_body(factor, g_ref, q_ref, k_ref, v_ref, l_ref, gk_ref, gv_ref):
    keep = causal(g_ref.shape[0])
    for h, s in head_slices():
        g, q, k, v, later = g_ref[:, s], q_ref[:, s], k_ref[:, s], v_ref[:, s], l_ref[h]
        scores = jnp.where(keep, dot(q, k, 1, 1), 0.0).astype(BF16)
        reverse = jnp.where(keep, dot(g, v, 1, 1), 0.0).astype(BF16)
        gk_ref[:, s] = (factor * (dot(v, later, 1, 1) + dot(reverse, q, 0, 0))).astype(BF16)
        gv_ref[:, s] = (factor * (dot(k, later, 1, 0) + dot(scores, g, 0, 0))).astype(BF16)


def block(at, k, size):
    return pl.ds(pl.multiple_of(lax.rem(at + k, 4) * size, size), size)


def half_a(at_ref, width):
    return pl.ds(pl.multiple_of(at_ref[0] * width, width), width // 2)


def block_b(at_ref, k, width):
    start = at_ref[0] * width + width // 2 + lax.rem(at_ref[1] + k, 4) * (width // 8)
    return pl.ds(pl.multiple_of(start, width // 8), width // 8)


def other_b(at_ref, k, width):
    start = width // 2 + lax.rem(at_ref[1] + k, 4) * (width // 8)
    return pl.ds(pl.multiple_of(start, width // 8), width // 8)


def own_b(at_ref, width):
    return pl.ds(pl.multiple_of(at_ref[0] * width + width // 2, width // 2), width // 2)


def weight_y_body(at_ref, mine_ref, theirs_ref, og_ref, oog_ref, *o_refs):
    width = oog_ref.shape[1]
    og = jnp.concatenate([og_ref[:, block_b(at_ref, k, width)] for k in range(4)], axis=1)
    oog = jnp.concatenate([oog_ref[:, other_b(at_ref, k, width)] for k in range(4)], axis=1)
    step = 256

    def body(r, carry):
        rows = pl.ds(pl.multiple_of(r * step, step), step)
        both = dot(mine_ref[rows, :], og, 1, 0) + dot(theirs_ref[rows, :], oog, 1, 0)
        for k in range(4):
            o_refs[k][rows, :] = both[:, k * (width // 8) : (k + 1) * (width // 8)].astype(BF16)
        return carry

    lax.fori_loop(0, mine_ref.shape[0] // step, body, 0)


def weight_x_body(at_ref, mine_ref, theirs_ref, og_ref, oog_ref, *o_refs):
    width = oog_ref.shape[1]
    og = og_ref[:, half_a(at_ref, width)]
    oog = oog_ref[:, : width // 2]
    step = 256
    size = o_refs[0].shape[0]
    for k in range(4):
        start = lax.rem(at_ref[2] + k, 4) * size

        def body(r, carry, start=start, k=k):
            rows = pl.ds(pl.multiple_of(start + r * step, step), step)
            both = dot(mine_ref[rows, :], og, 1, 0) + dot(theirs_ref[rows, :], oog, 1, 0)
            o_refs[k][pl.ds(pl.multiple_of(r * step, step), step), :] = both.astype(BF16)
            return carry

        lax.fori_loop(0, size // step, body, 0)


def added(refs):
    total = refs[0][...].astype(F32)
    for ref in refs[1:]:
        total = total + ref[...].astype(F32)
    return total


def add_then_x_body(at_ref, *refs):
    size = refs[0].shape[0] // 4
    for k in range(4):
        rows = block(at_ref[2], k, size)
        total = refs[0][rows, :].astype(F32)
        for ref in refs[1:4]:
            total = total + ref[rows, :].astype(F32)
        refs[4 + k][...] = total.astype(BF16)


def add_then_y_body(at_ref, *refs):
    size = refs[0].shape[1] // 4
    for k in range(4):
        columns = block(at_ref[1], k, size)
        total = refs[0][:, columns].astype(F32)
        for ref in refs[1:4]:
            total = total + ref[:, columns].astype(F32)
        refs[4 + k][...] = total.astype(BF16)


def add_then_zl_body(at_ref, *refs):
    low = at_ref[4] == 0
    via_x, via_y = added(refs[:4]), added(refs[4:8])
    refs[8][...] = jnp.where(low, via_x, via_y).astype(BF16)
    refs[9][...] = jnp.where(low, via_y, via_x).astype(BF16)


def add_then_zh_body(at_ref, a_ref, b_ref, *o_refs):
    size = a_ref.shape[0] // 4
    for k in range(4):
        rows = block(at_ref[3], k, size)
        o_refs[k][...] = (a_ref[rows, :].astype(F32) + b_ref[rows, :].astype(F32)).astype(BF16)


def add_then_all_body(*refs):
    total = added(refs[:4]).astype(BF16)
    for n in range(refs[4].shape[0]):
        refs[4][n] = total


def finish_weight_body(scale, i_ref, o_ref):
    for n in range(i_ref.shape[0]):
        y, zl, core = n // 4, n // 2 % 2, n % 2
        column = (core * 8 + (1 - zl) * 4 + y) * i_ref.shape[2]
        o_ref[:, column : column + i_ref.shape[2]] = i_ref[n].astype(F32) * scale


def place_body(at_ref, *refs):
    size = refs[0].shape[0]
    for k in range(4):
        refs[4][block(at_ref[3], k, size), :] = refs[k][...]


def stack_body(*refs):
    size = refs[0].shape[0]
    for k in range(4):
        refs[4][k * size : (k + 1) * size, :] = refs[k][...]


def projected_body(other, at_ref, og_ref, *refs):
    a_refs, b_refs, o_ref = refs[:4], refs[4:8], refs[8]
    if other:
        width = og_ref.shape[1]
        parts = [og_ref[:, : width // 2]] + [og_ref[:, other_b(at_ref, k, width)] for k in range(4)]
    else:
        width = og_ref.shape[1] // 2
        parts = [og_ref[:, half_a(at_ref, width)]] + [og_ref[:, block_b(at_ref, k, width)] for k in range(4)]
    rows = jnp.concatenate(parts, axis=1)
    size = a_refs[0].shape[0]
    for k in range(4):
        weight = jnp.concatenate(
            [a_refs[k][...]] + [b[k * size : (k + 1) * size, :] for b in b_refs], axis=1
        )
        o_ref[:, k * size : (k + 1) * size] = dot(rows, weight, 1, 1)


def grad_attn_body(at_ref, mine_ref, theirs_ref, o_ref):
    size = mine_ref.shape[1] // 4
    for k in range(4):
        s = slice(k * size, (k + 1) * size)
        o_ref[:, block(at_ref[2], k, size)] = (mine_ref[:, s] + theirs_ref[:, s]).astype(BF16)


def local(queries, keys, values, out_weight, out_grad):
    q, k, v, og = queries[0], keys[0], values[0], out_grad[0]
    tokens, inner = q.shape
    width = og.shape[1] // 2
    ctx, fsdp = lax.axis_index("ctx"), lax.axis_index("fsdp")
    y, zl, core = ctx // 4, ctx // 2 % 2, ctx % 2
    x, zh = fsdp // 4, fsdp % 4
    at = jnp.stack([core, y, x, zh, zl]).astype(jnp.int32)
    factor = (HEAD * tokens * lax.axis_size("ctx")) ** (-0.5)
    scale = (tokens * lax.axis_size("ctx") * lax.axis_size("fsdp")) ** (-0.5)
    rows = rows_spec(tokens)
    heads = (HEADS // PER,)
    token_flops = 2 * tokens * inner * HEAD

    oog = from_core(lax.dynamic_slice(og, (0, (1 - core) * width), (tokens, width)))

    key_states = call(
        states_body, shape((HEADS, HEAD, HEAD)), k, v,
        grid=heads, in_specs=[rows, rows], out_specs=STATE_SPEC, flops=token_flops, name="key_states",
    )

    def exchange(states, reverse, name):
        by_head = lax.all_to_all(states, "ctx", 0, 0)
        sums = call(functools.partial(scan_body, reverse), shape(by_head.shape), by_head, flops=by_head.size, name=name)
        return lax.all_to_all(sums, "ctx", 0, 0)

    prior = exchange(key_states, False, "prior_scan")

    wa = lax.dynamic_slice(out_weight, (0, core * width), (out_weight.shape[0], width // 2))
    wb = lax.dynamic_slice(
        out_weight, (0, core * width + width // 2 + y * (width // 8)), (out_weight.shape[0], width // 8)
    )
    zb = [wb] + [from_zh(wb, n) for n in (1, 2, 3)]
    za = [wa] + [from_zh(wa, n) for n in (1, 2, 3)]
    z_rows = 4 * out_weight.shape[0]
    wb = call(place_body, shape((z_rows, wb.shape[1])), at, *zb, name="place_b")
    xb = [wb] + [from_x(wb, n) for n in (1, 2, 3)]
    wa = call(place_body, shape((z_rows, wa.shape[1])), at, *za, name="place_a")
    xa = [wa] + [from_x(wa, n) for n in (1, 2, 3)]
    wb = call(stack_body, shape((inner, wb.shape[1])), *xb, name="stack_b")
    yb = [wb] + [from_y(wb, n) for n in (1, 2, 3)]

    attended = call(
        functools.partial(attended_body, factor), shape((inner, tokens)), q, k, v, prior,
        grid=heads, in_specs=[rows, rows, rows, STATE_SPEC],
        out_specs=pl.BlockSpec((PER * HEAD, tokens), lambda i: (i, 0)), flops=5 * token_flops, name="attended",
    )
    partner = from_core(attended)
    gw_flops = 2 * inner * 2 * tokens * (width // 2)
    gy = call(weight_y_body, [shape((inner, width // 8))] * 4, at, attended, partner, og, oog, flops=gw_flops, name="weight_y")
    gy = [gy[0]] + [from_y(gy[n], 4 - n) for n in (1, 2, 3)]
    gx = call(weight_x_body, [shape((inner // 4, width // 2))] * 4, at, attended, partner, og, oog, flops=gw_flops, name="weight_x")
    gx = [gx[0]] + [from_x(gx[n], 4 - n) for n in (1, 2, 3)]

    project_flops = 2 * tokens * inner * width
    for_partner = call(
        functools.partial(projected_body, True), shape((tokens, inner), F32), at, oog, *xa, *yb, flops=project_flops, name="project_other"
    )
    from_partner = from_core(for_partner)
    mine = call(
        functools.partial(projected_body, False), shape((tokens, inner), F32), at, og, *xa, *yb, flops=project_flops, name="project_own"
    )
    ga = call(grad_attn_body, shape((tokens, inner)), at, mine, from_partner, name="grad_attn")
    grad_states = call(
        states_body, shape((HEADS, HEAD, HEAD)), q, ga,
        grid=heads, in_specs=[rows, rows], out_specs=STATE_SPEC, flops=token_flops, name="grad_states",
    )
    later = exchange(grad_states, True, "later_scan")

    quarter = shape((inner // 4, width // 8))
    gyx = call(add_then_x_body, [quarter] * 4, at, *gy, name="add_then_x")
    gyx = [gyx[0]] + [from_x(gyx[n], 4 - n) for n in (1, 2, 3)]
    gxy = call(add_then_y_body, [quarter] * 4, at, *gx, name="add_then_y")
    gxy = [gxy[0]] + [from_y(gxy[n], 4 - n) for n in (1, 2, 3)]
    keep, give = call(add_then_zl_body, [quarter] * 2, at, *gyx, *gxy, name="add_then_zl")
    block_shape = shape((inner // 16, width // 8))
    gz = call(add_then_zh_body, [block_shape] * 4, at, keep, from_zl(give), name="add_then_zh")
    gz = [gz[0]] + [from_zh(gz[n], 4 - n) for n in (1, 2, 3)]
    spread = call(add_then_all_body, shape((16, inner // 16, width // 8)), *gz, name="add_then_all")
    gathered = lax.all_to_all(spread, "ctx", 0, 0)
    grad_weight = call(
        functools.partial(finish_weight_body, scale), shape((inner // 16, 2 * width), F32), gathered, name="finish_weight"
    )

    grad_queries = call(
        functools.partial(grad_queries_body, factor), shape((tokens, inner)), ga, k, v, prior,
        grid=heads, in_specs=[rows, rows, rows, STATE_SPEC], out_specs=rows, flops=5 * token_flops, name="grad_queries",
    )
    grad_keys, grad_values = call(
        functools.partial(grad_keys_values_body, factor), [shape((tokens, inner))] * 2, ga, q, k, v, later,
        grid=heads, in_specs=[rows, rows, rows, rows, STATE_SPEC], out_specs=[rows, rows], flops=10 * token_flops, name="grad_keys_values",
    )
    return grad_queries[None], grad_keys[None], grad_values[None], grad_weight


def solution(mesh):
    in_specs = (
        P("fsdp", "ctx", None),
        P("fsdp", "ctx", None),
        P("fsdp", "ctx", None),
        P("fsdp", None),
        P("fsdp", "ctx", None),
    )
    out_specs = (
        P("fsdp", "ctx", None),
        P("fsdp", "ctx", None),
        P("fsdp", "ctx", None),
        P("fsdp", None),
    )
    return jax.shard_map(local, mesh=mesh, in_specs=in_specs, out_specs=out_specs, check_vma=False)
```

```python
import functools

import jax
import jax.numpy as jnp
from jax import lax
from jax.experimental import pallas as pl
from jax.experimental.pallas import tpu as pltpu
from jax.sharding import PartitionSpec as P

HEADS = 16
HEAD = 128
F32 = jnp.float32
BF16 = jnp.bfloat16


def dot(a, b, da, db):
    return lax.dot_general(a, b, (((da,), (db,)), ((), ())), preferred_element_type=F32)


AXES = ("y", "zl", "c", "x", "zh")
CTX, FSDP = AXES[:3], AXES[3:]


def from_core(v):
    return lax.ppermute(v, "c", [(0, 1), (1, 0)])


def copies(v, axis):
    return [v] + [lax.ppermute(v, axis, [((i + k) % 4, i) for i in range(4)]) for k in (1, 2, 3)]


def spread(pieces, axis):
    return [pieces[0]] + [
        lax.ppermute(pieces[k], axis, [(i, (i + k) % 4) for i in range(4)]) for k in (1, 2, 3)
    ]


def call(body, out, *args, grid=None, in_specs=None, out_specs=None, flops=0, room=None):
    size = sum(a.size * a.dtype.itemsize for a in args)
    outs = out if isinstance(out, (tuple, list)) else [out]
    size += sum(o.size * jnp.dtype(o.dtype).itemsize for o in outs)
    kwargs = {}
    if grid is not None:
        kwargs = dict(grid=grid)
    else:
        full = pl.BlockSpec(memory_space=pltpu.VMEM)
        small = pl.BlockSpec(memory_space=pltpu.SMEM)
        in_specs = [small if a.dtype == jnp.int32 else full for a in args]
        out_specs = jax.tree.map(lambda o: full, out)
    if room is None:
        room = 2 * size + 8 * 2**20
    return pl.pallas_call(
        body,
        out_shape=out,
        in_specs=list(in_specs),
        out_specs=out_specs,
        cost_estimate=pl.CostEstimate(flops=flops, bytes_accessed=size, transcendentals=0),
        compiler_params=pltpu.CompilerParams(vmem_limit_bytes=min(room, 56 * 2**20)),
        **kwargs,
    )(*args)


def shape(dims, dtype=BF16):
    return jax.ShapeDtypeStruct(dims, dtype)


PER = 4


def head_slices():
    return [(h, slice(h * HEAD, (h + 1) * HEAD)) for h in range(PER)]


def rows_spec(tokens):
    return pl.BlockSpec((tokens, PER * HEAD), lambda i: (0, i))


STATE_SPEC = pl.BlockSpec((PER, HEAD, HEAD), lambda i: (i, 0, 0))


def states_body(a_ref, b_ref, o_ref):
    for h, s in head_slices():
        o_ref[h] = dot(a_ref[:, s], b_ref[:, s], 0, 0).astype(BF16)


def scan_body(reverse, i_ref, o_ref):
    count = i_ref.shape[0]
    total = jnp.zeros(i_ref.shape[1:], F32)
    for n in range(count):
        at = count - 1 - n if reverse else n
        o_ref[at] = total.astype(BF16)
        total = total + i_ref[at].astype(F32)


def causal(tokens):
    return lax.broadcasted_iota(jnp.int32, (tokens, tokens), 0) >= lax.broadcasted_iota(
        jnp.int32, (tokens, tokens), 1
    )


def attended_body(factor, q_ref, k_ref, v_ref, p_ref, o_ref):
    keep = causal(q_ref.shape[0])
    for h, s in head_slices():
        q = q_ref[:, s]
        scores = jnp.where(keep, dot(q, k_ref[:, s], 1, 1), 0.0).astype(BF16)
        o_ref[s, :] = (factor * (dot(p_ref[h], q, 0, 1) + dot(v_ref[:, s], scores, 0, 1))).astype(BF16)


def grad_queries_body(factor, g_ref, k_ref, v_ref, p_ref, o_ref):
    keep = causal(g_ref.shape[0])
    for h, s in head_slices():
        g = g_ref[:, s]
        reverse = jnp.where(keep, dot(g, v_ref[:, s], 1, 1), 0.0).astype(BF16)
        o_ref[:, s] = (factor * (dot(g, p_ref[h], 1, 1) + dot(reverse, k_ref[:, s], 1, 0))).astype(BF16)


def grad_keys_values_body(factor, g_ref, q_ref, k_ref, v_ref, l_ref, gk_ref, gv_ref):
    keep = causal(g_ref.shape[0])
    for h, s in head_slices():
        g, q, k, v, later = g_ref[:, s], q_ref[:, s], k_ref[:, s], v_ref[:, s], l_ref[h]
        scores = jnp.where(keep, dot(q, k, 1, 1), 0.0).astype(BF16)
        reverse = jnp.where(keep, dot(g, v, 1, 1), 0.0).astype(BF16)
        gk_ref[:, s] = (factor * (dot(v, later, 1, 1) + dot(reverse, q, 0, 0))).astype(BF16)
        gv_ref[:, s] = (factor * (dot(k, later, 1, 0) + dot(scores, g, 0, 0))).astype(BF16)


def block(at, k, size):
    return pl.ds(pl.multiple_of(lax.rem(at + k, 4) * size, size), size)


def half_a(at_ref, width):
    return pl.ds(pl.multiple_of(at_ref[0] * width, width), width // 2)


def block_b(at_ref, k, width):
    start = at_ref[0] * width + width // 2 + lax.rem(at_ref[1] + k, 4) * (width // 8)
    return pl.ds(pl.multiple_of(start, width // 8), width // 8)


def other_b(at_ref, k, width):
    start = width // 2 + lax.rem(at_ref[1] + k, 4) * (width // 8)
    return pl.ds(pl.multiple_of(start, width // 8), width // 8)


def weight_y_body(at_ref, mine_ref, theirs_ref, og_ref, oog_ref, *o_refs):
    width = oog_ref.shape[1]
    og = jnp.concatenate([og_ref[:, block_b(at_ref, k, width)] for k in range(4)], axis=1)
    oog = jnp.concatenate([oog_ref[:, other_b(at_ref, k, width)] for k in range(4)], axis=1)
    step = 512

    def body(r, carry):
        rows = pl.ds(pl.multiple_of(r * step, step), step)
        both = dot(mine_ref[rows, :], og, 1, 0) + dot(theirs_ref[rows, :], oog, 1, 0)
        for k in range(4):
            o_refs[k][rows, :] = both[:, k * (width // 8) : (k + 1) * (width // 8)].astype(BF16)
        return carry

    lax.fori_loop(0, mine_ref.shape[0] // step, body, 0)


def weight_x_body(at_ref, mine_ref, theirs_ref, og_ref, oog_ref, *o_refs):
    width = oog_ref.shape[1]
    og = og_ref[:, half_a(at_ref, width)]
    oog = oog_ref[:, : width // 2]
    step = 512
    size = o_refs[0].shape[0]
    for k in range(4):
        start = lax.rem(at_ref[2] + k, 4) * size

        def body(r, carry, start=start, k=k):
            rows = pl.ds(pl.multiple_of(start + r * step, step), step)
            both = dot(mine_ref[rows, :], og, 1, 0) + dot(theirs_ref[rows, :], oog, 1, 0)
            o_refs[k][pl.ds(pl.multiple_of(r * step, step), step), :] = both.astype(BF16)
            return carry

        lax.fori_loop(0, size // step, body, 0)


def added(refs):
    total = refs[0][...].astype(F32)
    for ref in refs[1:]:
        total = total + ref[...].astype(F32)
    return total


def add_then_x_body(at_ref, *refs):
    size = refs[0].shape[0] // 4
    for k in range(4):
        rows = block(at_ref[2], k, size)
        total = refs[0][rows, :].astype(F32)
        for ref in refs[1:4]:
            total = total + ref[rows, :].astype(F32)
        refs[4 + k][...] = total.astype(BF16)


def add_then_y_body(at_ref, *refs):
    size = refs[0].shape[1] // 4
    for k in range(4):
        columns = block(at_ref[1], k, size)
        total = refs[0][:, columns].astype(F32)
        for ref in refs[1:4]:
            total = total + ref[:, columns].astype(F32)
        refs[4 + k][...] = total.astype(BF16)


def add_then_z_body(*refs):
    size = refs[8].shape[1]
    for first, total in ((0, added(refs[:4])), (4, added(refs[4:8]))):
        for n in range(4):
            refs[8][first + n] = total[n * size : (n + 1) * size, :].astype(BF16)


def add_then_all_body(i_ref, o_ref):
    total = added([i_ref.at[n] for n in range(i_ref.shape[0])]).astype(BF16)
    for n in range(o_ref.shape[0]):
        o_ref[n] = total


def finish_weight_body(scale, i_ref, o_ref):
    for n in range(i_ref.shape[0]):
        y, zl, core = n // 4, n // 2 % 2, n % 2
        column = (core * 8 + (1 - zl) * 4 + y) * i_ref.shape[2]
        o_ref[:, column : column + i_ref.shape[2]] = i_ref[n].astype(F32) * scale


def place_body(at_ref, *refs):
    size = refs[0].shape[0]
    for k in range(4):
        refs[4][block(at_ref[3], k, size), :] = refs[k][...]


def projected_body(other, at_ref, og_ref, a0, a1, a2, a3, b0, b1, b2, b3, o_ref):
    if other:
        width = og_ref.shape[1]
        parts = [og_ref[:, : width // 2]] + [og_ref[:, other_b(at_ref, k, width)] for k in range(4)]
    else:
        width = og_ref.shape[1] // 2
        parts = [og_ref[:, half_a(at_ref, width)]] + [og_ref[:, block_b(at_ref, k, width)] for k in range(4)]
    rows = jnp.concatenate(parts, axis=1)
    for k, a_ref in enumerate((a0, a1, a2, a3)):
        s = block(at_ref[2], k, a_ref.shape[0])
        weight = jnp.concatenate([a_ref[...]] + [b[s, :] for b in (b0, b1, b2, b3)], axis=1)
        o_ref[:, s] = dot(rows, weight, 1, 1)


def grad_attn_body(mine_ref, theirs_ref, q_ref, g_ref, o_ref):
    g_ref[...] = (mine_ref[...] + theirs_ref[...]).astype(BF16)
    for h, s in head_slices():
        o_ref[h] = dot(q_ref[:, s], g_ref[:, s], 0, 0).astype(BF16)


def local(queries, keys, values, out_weight, out_grad):
    q, k, v, og = queries[0], keys[0], values[0], out_grad[0]
    tokens, inner = q.shape
    width = og.shape[1] // 2
    y, _, core, x, zh = [lax.axis_index(name) for name in AXES]
    at = jnp.stack([core, y, x, zh]).astype(jnp.int32)
    factor = (HEAD * tokens * 16) ** (-0.5)
    scale = (tokens * 16 * 16) ** (-0.5)
    rows = rows_spec(tokens)
    heads = (HEADS // PER,)
    token_flops = 2 * tokens * inner * HEAD

    oog = from_core(lax.dynamic_slice(og, (0, (1 - core) * width), (tokens, width)))

    key_states = call(
        states_body, shape((HEADS, HEAD, HEAD)), k, v,
        grid=heads, in_specs=[rows, rows], out_specs=STATE_SPEC, flops=token_flops,
    )

    def exchange(states, reverse):
        by_head = lax.all_to_all(states, CTX, 0, 0)
        sums = call(functools.partial(scan_body, reverse), shape(by_head.shape), by_head, flops=by_head.size)
        return lax.all_to_all(sums, CTX, 0, 0)

    wa = lax.dynamic_slice(out_weight, (0, core * width), (out_weight.shape[0], width // 2))
    wb = lax.dynamic_slice(
        out_weight, (0, core * width + width // 2 + y * (width // 8)), (out_weight.shape[0], width // 8)
    )
    za = copies(wa, "zh")
    wb = lax.all_to_all(jnp.broadcast_to(wb[None], (16, *wb.shape)), FSDP, 0, 0).reshape(inner, -1)
    yb = copies(wb, "y")
    wa = call(place_body, shape((4 * out_weight.shape[0], wa.shape[1])), at, *za)
    xa = copies(wa, "x")
    prior = exchange(key_states, False)

    attended = call(
        functools.partial(attended_body, factor), shape((inner, tokens)), q, k, v, prior,
        grid=heads, in_specs=[rows, rows, rows, STATE_SPEC],
        out_specs=pl.BlockSpec((PER * HEAD, tokens), lambda i: (i, 0)), flops=5 * token_flops,
    )
    partner = from_core(attended)

    project_flops = 2 * tokens * inner * width
    for_partner = call(
        functools.partial(projected_body, True), shape((tokens, inner), F32), at, oog, *xa, *yb,
        flops=project_flops,
    )
    from_partner = from_core(for_partner)

    gw_flops = 2 * inner * 2 * tokens * (width // 2)
    gy = call(
        weight_y_body, [shape((inner, width // 8))] * 4, at, attended, partner, og, oog,
        flops=gw_flops,
    )
    gx = call(
        weight_x_body, [shape((inner // 4, width // 2))] * 4, at, attended, partner, og, oog,
        flops=gw_flops,
    )
    mine = call(
        functools.partial(projected_body, False), shape((tokens, inner), F32), at, og, *xa, *yb,
        flops=project_flops,
    )
    gy = spread(gy, "y")
    gx = spread(gx, "x")
    ga, grad_states = call(
        grad_attn_body, [shape((tokens, inner)), shape((HEADS, HEAD, HEAD))], mine, from_partner, q,
        grid=heads, in_specs=[rows, rows, rows], out_specs=[rows, STATE_SPEC], flops=token_flops,
    )
    quarter = shape((inner // 4, width // 8))
    gyx = call(add_then_x_body, [quarter] * 4, at, *gy)
    gyx = spread(gyx, "x")
    later = exchange(grad_states, True)
    gxy = call(add_then_y_body, [quarter] * 4, at, *gx)
    gxy = spread(gxy, "y")
    grad_queries = call(
        functools.partial(grad_queries_body, factor), shape((tokens, inner)), ga, k, v, prior,
        grid=heads, in_specs=[rows, rows, rows, STATE_SPEC], out_specs=rows, flops=5 * token_flops,
    )
    gz = call(add_then_z_body, shape((8, inner // 16, width // 8)), *gyx, *gxy)
    grad_keys, grad_values = call(
        functools.partial(grad_keys_values_body, factor), [shape((tokens, inner))] * 2, ga, q, k, v, later,
        grid=heads, in_specs=[rows, rows, rows, rows, STATE_SPEC], out_specs=[rows, rows], flops=10 * token_flops,
    )
    gz = lax.all_to_all(gz, ("zl", "zh"), 0, 0)
    total = call(add_then_all_body, shape((16, inner // 16, width // 8)), gz)
    gathered = lax.all_to_all(total, CTX, 0, 0)
    grad_weight = call(functools.partial(finish_weight_body, scale), shape((inner // 16, 2 * width), F32), gathered)

    return grad_queries[None], grad_keys[None], grad_values[None], grad_weight


def solution(mesh):
    fine = jax.sharding.Mesh(mesh.devices.reshape(4, 2, 2, 4, 4), AXES)
    tokens, rows = P(FSDP, CTX, None), P(FSDP, None)

    return jax.shard_map(
        local, mesh=fine, in_specs=(tokens, tokens, tokens, rows, tokens), out_specs=(tokens, tokens, tokens, rows), check_vma=False
    )
```

```python
import functools

import jax
import jax.numpy as jnp
from jax import lax
from jax.experimental import pallas as pl
from jax.experimental.pallas import tpu as pltpu
from jax.sharding import PartitionSpec as P

HEADS = 16
HEAD = 128
F32 = jnp.float32
BF16 = jnp.bfloat16


def dot(a, b, da, db):
    return lax.dot_general(a, b, (((da,), (db,)), ((), ())), preferred_element_type=F32)


AXES = ("y", "zl", "c", "x", "zh")
CTX, FSDP = AXES[:3], AXES[3:]


def from_core(v):
    return lax.ppermute(v, "c", [(0, 1), (1, 0)])


def copies(v, axis):
    return [v] + [lax.ppermute(v, axis, [((i + k) % 4, i) for i in range(4)]) for k in (1, 2, 3)]


def spread(pieces, axis):
    return [pieces[0]] + [
        lax.ppermute(pieces[k], axis, [(i, (i + k) % 4) for i in range(4)]) for k in (1, 2, 3)
    ]


def call(body, out, *args, grid=None, in_specs=None, out_specs=None, flops=0, room=None):
    size = sum(a.size * a.dtype.itemsize for a in args)
    outs = out if isinstance(out, (tuple, list)) else [out]
    size += sum(o.size * jnp.dtype(o.dtype).itemsize for o in outs)
    kwargs = {}
    if grid is not None:
        kwargs = dict(grid=grid)
    else:
        full = pl.BlockSpec(memory_space=pltpu.VMEM)
        small = pl.BlockSpec(memory_space=pltpu.SMEM)
        in_specs = [small if a.dtype == jnp.int32 else full for a in args]
        out_specs = jax.tree.map(lambda o: full, out)
    if room is None:
        room = size + 6 * 2**20
    return pl.pallas_call(
        body,
        out_shape=out,
        in_specs=list(in_specs),
        out_specs=out_specs,
        cost_estimate=pl.CostEstimate(flops=flops, bytes_accessed=size, transcendentals=0),
        compiler_params=pltpu.CompilerParams(vmem_limit_bytes=min(room, 56 * 2**20)),
        **kwargs,
    )(*args)


def shape(dims, dtype=BF16):
    return jax.ShapeDtypeStruct(dims, dtype)


PER = 4


def head_slices():
    return [(h, slice(h * HEAD, (h + 1) * HEAD)) for h in range(PER)]


def rows_spec(tokens):
    return pl.BlockSpec((tokens, PER * HEAD), lambda i: (0, i))


STATE_SPEC = pl.BlockSpec((PER, HEAD, HEAD), lambda i: (i, 0, 0))


def states_body(a_ref, b_ref, o_ref):
    for h, s in head_slices():
        o_ref[h] = dot(a_ref[:, s], b_ref[:, s], 0, 0).astype(BF16)


def scan_body(reverse, i_ref, o_ref):
    count = i_ref.shape[0]
    total = jnp.zeros(i_ref.shape[1:], F32)
    for n in range(count):
        at = count - 1 - n if reverse else n
        o_ref[at] = total.astype(BF16)
        total = total + i_ref[at].astype(F32)


def causal(tokens):
    return lax.broadcasted_iota(jnp.int32, (tokens, tokens), 0) >= lax.broadcasted_iota(
        jnp.int32, (tokens, tokens), 1
    )


def attended_body(factor, q_ref, k_ref, v_ref, p_ref, o_ref):
    keep = causal(q_ref.shape[0])
    for h, s in head_slices():
        q = q_ref[:, s]
        scores = jnp.where(keep, dot(q, k_ref[:, s], 1, 1), 0.0).astype(BF16)
        o_ref[s, :] = (factor * (dot(p_ref[h], q, 0, 1) + dot(v_ref[:, s], scores, 0, 1))).astype(BF16)


def grad_queries_body(factor, g_ref, k_ref, v_ref, p_ref, o_ref):
    keep = causal(g_ref.shape[0])
    for h, s in head_slices():
        g = g_ref[:, s]
        reverse = jnp.where(keep, dot(g, v_ref[:, s], 1, 1), 0.0).astype(BF16)
        o_ref[:, s] = (factor * (dot(g, p_ref[h], 1, 1) + dot(reverse, k_ref[:, s], 1, 0))).astype(BF16)


def grad_keys_values_body(factor, g_ref, q_ref, k_ref, v_ref, l_ref, gk_ref, gv_ref):
    keep = causal(g_ref.shape[0])
    for h, s in head_slices():
        g, q, k, v, later = g_ref[:, s], q_ref[:, s], k_ref[:, s], v_ref[:, s], l_ref[h]
        scores = jnp.where(keep, dot(q, k, 1, 1), 0.0).astype(BF16)
        reverse = jnp.where(keep, dot(g, v, 1, 1), 0.0).astype(BF16)
        gk_ref[:, s] = (factor * (dot(v, later, 1, 1) + dot(reverse, q, 0, 0))).astype(BF16)
        gv_ref[:, s] = (factor * (dot(k, later, 1, 0) + dot(scores, g, 0, 0))).astype(BF16)


def block(at, k, size):
    return pl.ds(pl.multiple_of(lax.rem(at + k, 4) * size, size), size)


def half_a(at_ref, width):
    return pl.ds(pl.multiple_of(at_ref[0] * width, width), width // 2)


def block_b(at_ref, k, width):
    start = at_ref[0] * width + width // 2 + lax.rem(at_ref[1] + k, 4) * (width // 8)
    return pl.ds(pl.multiple_of(start, width // 8), width // 8)


def other_b(at_ref, k, width):
    start = width // 2 + lax.rem(at_ref[1] + k, 4) * (width // 8)
    return pl.ds(pl.multiple_of(start, width // 8), width // 8)


def weight_y_body(at_ref, mine_ref, theirs_ref, og_ref, oog_ref, *o_refs):
    width = oog_ref.shape[1]
    og = jnp.concatenate([og_ref[:, block_b(at_ref, k, width)] for k in range(4)], axis=1)
    oog = jnp.concatenate([oog_ref[:, other_b(at_ref, k, width)] for k in range(4)], axis=1)
    step = 512

    def body(r, carry):
        rows = pl.ds(pl.multiple_of(r * step, step), step)
        both = dot(mine_ref[rows, :], og, 1, 0) + dot(theirs_ref[rows, :], oog, 1, 0)
        for k in range(4):
            o_refs[k][rows, :] = both[:, k * (width // 8) : (k + 1) * (width // 8)].astype(BF16)
        return carry

    lax.fori_loop(0, mine_ref.shape[0] // step, body, 0)


def weight_x_body(at_ref, mine_ref, theirs_ref, og_ref, oog_ref, *o_refs):
    width = oog_ref.shape[1]
    og = og_ref[:, half_a(at_ref, width)]
    oog = oog_ref[:, : width // 2]
    step = 512
    size = o_refs[0].shape[0]
    for k in range(4):
        start = lax.rem(at_ref[2] + k, 4) * size

        def body(r, carry, start=start, k=k):
            rows = pl.ds(pl.multiple_of(start + r * step, step), step)
            both = dot(mine_ref[rows, :], og, 1, 0) + dot(theirs_ref[rows, :], oog, 1, 0)
            o_refs[k][pl.ds(pl.multiple_of(r * step, step), step), :] = both.astype(BF16)
            return carry

        lax.fori_loop(0, size // step, body, 0)


def added(refs):
    total = refs[0][...].astype(F32)
    for ref in refs[1:]:
        total = total + ref[...].astype(F32)
    return total


def add_then_x_body(at_ref, *refs):
    size = refs[0].shape[0] // 4
    for k in range(4):
        rows = block(at_ref[2], k, size)
        total = refs[0][rows, :].astype(F32)
        for ref in refs[1:4]:
            total = total + ref[rows, :].astype(F32)
        refs[4 + k][...] = total.astype(BF16)


def add_then_y_body(at_ref, *refs):
    size = refs[0].shape[1] // 4
    for k in range(4):
        columns = block(at_ref[1], k, size)
        total = refs[0][:, columns].astype(F32)
        for ref in refs[1:4]:
            total = total + ref[:, columns].astype(F32)
        refs[4 + k][...] = total.astype(BF16)


def add_then_z_body(at_ref, *refs):
    size = refs[8].shape[0]
    low = at_ref[4] == 0
    for k in range(4):
        s = block(at_ref[3], k, size)
        via_x, via_y = added([ref.at[s, :] for ref in refs[:4]]), added([ref.at[s, :] for ref in refs[4:8]])
        refs[8 + k][...] = jnp.where(low, via_x, via_y).astype(BF16)
        refs[12 + k][...] = jnp.where(low, via_y, via_x).astype(BF16)


def add_then_all_body(*refs):
    total = added(refs[:8]).astype(BF16)
    for n in range(refs[8].shape[0]):
        refs[8][n] = total


def finish_weight_body(scale, i_ref, o_ref):
    for n in range(i_ref.shape[0]):
        y, zl, core = n // 4, n // 2 % 2, n % 2
        column = (core * 8 + (1 - zl) * 4 + y) * i_ref.shape[2]
        o_ref[:, column : column + i_ref.shape[2]] = i_ref[n].astype(F32) * scale


def place_body(at_ref, *refs):
    size = refs[0].shape[0]
    for k in range(4):
        refs[4][block(at_ref[3], k, size), :] = refs[k][...]


def stack_body(at_ref, *refs):
    size = refs[0].shape[0]
    for k in range(4):
        refs[4][block(at_ref[2], k, size), :] = refs[k][...]


def projected_body(other, at_ref, og_ref, a0, a1, a2, a3, b0, b1, b2, b3, o_ref):
    if other:
        width = og_ref.shape[1]
        parts = [og_ref[:, : width // 2]] + [og_ref[:, other_b(at_ref, k, width)] for k in range(4)]
    else:
        width = og_ref.shape[1] // 2
        parts = [og_ref[:, half_a(at_ref, width)]] + [og_ref[:, block_b(at_ref, k, width)] for k in range(4)]
    rows = jnp.concatenate(parts, axis=1)
    for k, a_ref in enumerate((a0, a1, a2, a3)):
        s = block(at_ref[2], k, a_ref.shape[0])
        weight = jnp.concatenate([a_ref[...]] + [b[s, :] for b in (b0, b1, b2, b3)], axis=1)
        o_ref[:, s] = dot(rows, weight, 1, 1)


def grad_attn_body(mine_ref, theirs_ref, q_ref, g_ref, o_ref):
    g_ref[...] = (mine_ref[...] + theirs_ref[...]).astype(BF16)
    for h, s in head_slices():
        o_ref[h] = dot(q_ref[:, s], g_ref[:, s], 0, 0).astype(BF16)


def local(queries, keys, values, out_weight, out_grad):
    q, k, v, og = queries[0], keys[0], values[0], out_grad[0]
    tokens, inner = q.shape
    width = og.shape[1] // 2
    y, zl, core, x, zh = [lax.axis_index(name) for name in AXES]
    at = jnp.stack([core, y, x, zh, zl]).astype(jnp.int32)
    factor = (HEAD * tokens * 16) ** (-0.5)
    scale = (tokens * 16 * 16) ** (-0.5)
    rows = rows_spec(tokens)
    heads = (HEADS // PER,)
    token_flops = 2 * tokens * inner * HEAD

    oog = from_core(lax.dynamic_slice(og, (0, (1 - core) * width), (tokens, width)))

    key_states = call(
        states_body, shape((HEADS, HEAD, HEAD)), k, v,
        grid=heads, in_specs=[rows, rows], out_specs=STATE_SPEC, flops=token_flops,
    )

    def exchange(states, reverse):
        by_head = lax.all_to_all(states, CTX, 0, 0)
        sums = call(functools.partial(scan_body, reverse), shape(by_head.shape), by_head, flops=by_head.size)
        return lax.all_to_all(sums, CTX, 0, 0)

    wa = lax.dynamic_slice(out_weight, (0, core * width), (out_weight.shape[0], width // 2))
    wb = lax.dynamic_slice(
        out_weight, (0, core * width + width // 2 + y * (width // 8)), (out_weight.shape[0], width // 8)
    )
    za = copies(wa, "zh")
    zb = copies(wb, "zh")
    wb = call(place_body, shape((4 * out_weight.shape[0], wb.shape[1])), at, *zb)
    xb = copies(wb, "x")
    wb = call(stack_body, shape((inner, wb.shape[1])), at, *xb)
    yb = copies(wb, "y")
    wa = call(place_body, shape((4 * out_weight.shape[0], wa.shape[1])), at, *za)
    xa = copies(wa, "x")
    prior = exchange(key_states, False)

    attended = call(
        functools.partial(attended_body, factor), shape((inner, tokens)), q, k, v, prior,
        grid=heads, in_specs=[rows, rows, rows, STATE_SPEC],
        out_specs=pl.BlockSpec((PER * HEAD, tokens), lambda i: (i, 0)), flops=5 * token_flops,
    )
    partner = from_core(attended)

    gw_flops = 2 * inner * 2 * tokens * (width // 2)
    gy = call(
        weight_y_body, [shape((inner, width // 8))] * 4, at, attended, partner, og, oog,
        flops=gw_flops,
    )
    gx = call(
        weight_x_body, [shape((inner // 4, width // 2))] * 4, at, attended, partner, og, oog,
        flops=gw_flops,
    )
    project_flops = 2 * tokens * inner * width
    for_partner = call(
        functools.partial(projected_body, True), shape((tokens, inner), F32), at, oog, *xa, *yb,
        flops=project_flops,
    )
    from_partner = from_core(for_partner)

    mine = call(
        functools.partial(projected_body, False), shape((tokens, inner), F32), at, og, *xa, *yb,
        flops=project_flops,
    )
    gy = spread(gy, "y")
    gx = spread(gx, "x")
    ga, grad_states = call(
        grad_attn_body, [shape((tokens, inner)), shape((HEADS, HEAD, HEAD))], mine, from_partner, q,
        grid=heads, in_specs=[rows, rows, rows], out_specs=[rows, STATE_SPEC], flops=token_flops,
    )
    quarter = shape((inner // 4, width // 8))
    gyx = call(add_then_x_body, [quarter] * 4, at, *gy)
    gyx = spread(gyx, "x")
    later = exchange(grad_states, True)
    gxy = call(add_then_y_body, [quarter] * 4, at, *gx)
    gxy = spread(gxy, "y")
    grad_queries = call(
        functools.partial(grad_queries_body, factor), shape((tokens, inner)), ga, k, v, prior,
        grid=heads, in_specs=[rows, rows, rows, STATE_SPEC], out_specs=rows, flops=5 * token_flops,
    )
    gz = call(add_then_z_body, [shape((inner // 16, width // 8))] * 8, at, *gyx, *gxy)
    grad_keys, grad_values = call(
        functools.partial(grad_keys_values_body, factor), [shape((tokens, inner))] * 2, ga, q, k, v, later,
        grid=heads, in_specs=[rows, rows, rows, rows, STATE_SPEC], out_specs=[rows, rows], flops=10 * token_flops,
    )
    gz = [gz[0]] + [
        lax.ppermute(
            gz[n], ("zl", "zh"), [(i, (i // 4 ^ n // 4) * 4 + (i % 4 + n % 4) % 4) for i in range(8)]
        )
        for n in range(1, 8)
    ]
    total = call(add_then_all_body, shape((16, inner // 16, width // 8)), *gz)
    gathered = lax.all_to_all(total, CTX, 0, 0)
    grad_weight = call(functools.partial(finish_weight_body, scale), shape((inner // 16, 2 * width), F32), gathered)

    return grad_queries[None], grad_keys[None], grad_values[None], grad_weight


def solution(mesh):
    fine = jax.sharding.Mesh(mesh.devices.reshape(4, 2, 2, 4, 4), AXES)
    tokens, rows = P(FSDP, CTX, None), P(FSDP, None)

    return jax.shard_map(
        local, mesh=fine, in_specs=(tokens, tokens, tokens, rows, tokens), out_specs=(tokens, tokens, tokens, rows), check_vma=False
    )
```

```python
import functools

import jax
import jax.numpy as jnp
from jax import lax
from jax.experimental import pallas as pl
from jax.experimental.pallas import tpu as pltpu
from jax.sharding import PartitionSpec as P

HEADS = 16
HEAD = 128
F32 = jnp.float32
BF16 = jnp.bfloat16

ALL_ROOM = 60 * 2**20


def dot(a, b, da, db):
    return lax.dot_general(a, b, (((da,), (db,)), ((), ())), preferred_element_type=F32)


AXES = ("y", "zl", "c", "x", "zh")
CTX, FSDP = AXES[:3], AXES[3:]


def from_core(v):
    return lax.ppermute(v, "c", [(0, 1), (1, 0)])


def copies(v, axis):
    return [v] + [lax.ppermute(v, axis, [((i + k) % 4, i) for i in range(4)]) for k in (1, 2, 3)]


def spread(pieces, axis):
    return [pieces[0]] + [
        lax.ppermute(pieces[k], axis, [(i, (i + k) % 4) for i in range(4)]) for k in (1, 2, 3)
    ]


def call(body, out, *args, grid=None, in_specs=None, out_specs=None, flops=0, room=None):
    size = sum(a.size * a.dtype.itemsize for a in args)
    outs = out if isinstance(out, (tuple, list)) else [out]
    size += sum(o.size * jnp.dtype(o.dtype).itemsize for o in outs)
    kwargs = {}
    if grid is not None:
        kwargs = dict(grid=grid)
    else:
        full = pl.BlockSpec(memory_space=pltpu.VMEM)
        small = pl.BlockSpec(memory_space=pltpu.SMEM)
        in_specs = [small if a.dtype == jnp.int32 else full for a in args]
        out_specs = jax.tree.map(lambda o: full, out)
    if room is None:
        room = size + 6 * 2**20
    return pl.pallas_call(
        body,
        out_shape=out,
        in_specs=list(in_specs),
        out_specs=out_specs,
        cost_estimate=pl.CostEstimate(flops=flops, bytes_accessed=size, transcendentals=0),
        compiler_params=pltpu.CompilerParams(vmem_limit_bytes=room),
        **kwargs,
    )(*args)


def shape(dims, dtype=BF16):
    return jax.ShapeDtypeStruct(dims, dtype)


PER = 4


def head_slices():
    return [(h, slice(h * HEAD, (h + 1) * HEAD)) for h in range(PER)]


def rows_spec(tokens):
    return pl.BlockSpec((tokens, PER * HEAD), lambda i: (0, i))


STATE_SPEC = pl.BlockSpec((PER, HEAD, HEAD), lambda i: (i, 0, 0))


def states_body(a_ref, b_ref, o_ref):
    for h, s in head_slices():
        o_ref[h] = dot(a_ref[:, s], b_ref[:, s], 0, 0).astype(BF16)


def scan_body(reverse, i_ref, o_ref):
    count = i_ref.shape[0]
    total = jnp.zeros(i_ref.shape[1:], F32)
    for n in range(count):
        at = count - 1 - n if reverse else n
        o_ref[at] = total.astype(BF16)
        total = total + i_ref[at].astype(F32)


def causal(tokens):
    return lax.broadcasted_iota(jnp.int32, (tokens, tokens), 0) >= lax.broadcasted_iota(
        jnp.int32, (tokens, tokens), 1
    )


def attended_body(factor, q_ref, k_ref, v_ref, p_ref, o_ref):
    keep = causal(q_ref.shape[0])
    for h, s in head_slices():
        q = q_ref[:, s]
        scores = jnp.where(keep, dot(q, k_ref[:, s], 1, 1), 0.0).astype(BF16)
        o_ref[s, :] = (factor * (dot(p_ref[h], q, 0, 1) + dot(v_ref[:, s], scores, 0, 1))).astype(BF16)


def grad_queries_body(factor, g_ref, k_ref, v_ref, p_ref, o_ref):
    keep = causal(g_ref.shape[0])
    for h, s in head_slices():
        g = g_ref[:, s]
        reverse = jnp.where(keep, dot(g, v_ref[:, s], 1, 1), 0.0).astype(BF16)
        o_ref[:, s] = (factor * (dot(g, p_ref[h], 1, 1) + dot(reverse, k_ref[:, s], 1, 0))).astype(BF16)


def grad_keys_values_body(factor, g_ref, q_ref, k_ref, v_ref, l_ref, gk_ref, gv_ref):
    keep = causal(g_ref.shape[0])
    for h, s in head_slices():
        g, q, k, v, later = g_ref[:, s], q_ref[:, s], k_ref[:, s], v_ref[:, s], l_ref[h]
        scores = jnp.where(keep, dot(q, k, 1, 1), 0.0).astype(BF16)
        reverse = jnp.where(keep, dot(g, v, 1, 1), 0.0).astype(BF16)
        gk_ref[:, s] = (factor * (dot(v, later, 1, 1) + dot(reverse, q, 0, 0))).astype(BF16)
        gv_ref[:, s] = (factor * (dot(k, later, 1, 0) + dot(scores, g, 0, 0))).astype(BF16)


def block(at, k, size):
    return pl.ds(pl.multiple_of(lax.rem(at + k, 4) * size, size), size)


def half_a(at_ref, width):
    return pl.ds(pl.multiple_of(at_ref[0] * width, width), width // 2)


def block_b(at_ref, k, width):
    start = at_ref[0] * width + width // 2 + lax.rem(at_ref[1] + k, 4) * (width // 8)
    return pl.ds(pl.multiple_of(start, width // 8), width // 8)


def other_b(at_ref, k, width):
    start = width // 2 + lax.rem(at_ref[1] + k, 4) * (width // 8)
    return pl.ds(pl.multiple_of(start, width // 8), width // 8)


def weight_y_body(at_ref, mine_ref, theirs_ref, og_ref, oog_ref, *o_refs):
    width = oog_ref.shape[1]
    og = jnp.concatenate([og_ref[:, block_b(at_ref, k, width)] for k in range(4)], axis=1)
    oog = jnp.concatenate([oog_ref[:, other_b(at_ref, k, width)] for k in range(4)], axis=1)
    step = 512

    def body(r, carry):
        rows = pl.ds(pl.multiple_of(r * step, step), step)
        both = dot(mine_ref[rows, :], og, 1, 0) + dot(theirs_ref[rows, :], oog, 1, 0)
        for k in range(4):
            o_refs[k][rows, :] = both[:, k * (width // 8) : (k + 1) * (width // 8)].astype(BF16)
        return carry

    lax.fori_loop(0, mine_ref.shape[0] // step, body, 0)


def weight_x_body(at_ref, mine_ref, theirs_ref, og_ref, oog_ref, *o_refs):
    width = oog_ref.shape[1]
    og = og_ref[:, half_a(at_ref, width)]
    oog = oog_ref[:, : width // 2]
    step = 512
    size = o_refs[0].shape[0]
    for k in range(4):
        start = lax.rem(at_ref[2] + k, 4) * size

        def body(r, carry, start=start, k=k):
            rows = pl.ds(pl.multiple_of(start + r * step, step), step)
            both = dot(mine_ref[rows, :], og, 1, 0) + dot(theirs_ref[rows, :], oog, 1, 0)
            o_refs[k][pl.ds(pl.multiple_of(r * step, step), step), :] = both.astype(BF16)
            return carry

        lax.fori_loop(0, size // step, body, 0)


def added(refs):
    total = refs[0][...].astype(F32)
    for ref in refs[1:]:
        total = total + ref[...].astype(F32)
    return total


def add_then_x_body(at_ref, *refs):
    size = refs[0].shape[0] // 4
    for k in range(4):
        rows = block(at_ref[2], k, size)
        total = refs[0][rows, :].astype(F32)
        for ref in refs[1:4]:
            total = total + ref[rows, :].astype(F32)
        refs[4 + k][...] = total.astype(BF16)


def add_then_y_body(at_ref, *refs):
    size = refs[0].shape[1] // 4
    for k in range(4):
        columns = block(at_ref[1], k, size)
        total = refs[0][:, columns].astype(F32)
        for ref in refs[1:4]:
            total = total + ref[:, columns].astype(F32)
        refs[4 + k][...] = total.astype(BF16)


def add_then_z_body(*refs):
    size = refs[8].shape[1]
    for first, total in ((0, added(refs[:4])), (4, added(refs[4:8]))):
        for n in range(4):
            refs[8][first + n] = total[n * size : (n + 1) * size, :].astype(BF16)


def add_then_all_body(i_ref, o_ref):
    total = added([i_ref.at[n] for n in range(i_ref.shape[0])]).astype(BF16)
    for n in range(o_ref.shape[0]):
        o_ref[n] = total


def finish_weight_body(scale, i_ref, o_ref):
    for n in range(i_ref.shape[0]):
        y, zl, core = n // 4, n // 2 % 2, n % 2
        column = (core * 8 + (1 - zl) * 4 + y) * i_ref.shape[2]
        o_ref[:, column : column + i_ref.shape[2]] = i_ref[n].astype(F32) * scale


def place_body(at_ref, *refs):
    size, half = refs[0].shape[0], refs[4].shape[1]
    for k in range(4):
        s = block(at_ref[3], k, size)
        refs[4][s, :] = refs[k][:, :half]
        refs[5][s, :] = refs[k][:, half:]


def stack_body(at_ref, *refs):
    size = refs[0].shape[0]
    for k in range(4):
        refs[4][block(at_ref[2], k, size), :] = refs[k][...]


def projected_body(other, at_ref, og_ref, a0, a1, a2, a3, b0, b1, b2, b3, o_ref):
    if other:
        width = og_ref.shape[1]
        parts = [og_ref[:, : width // 2]] + [og_ref[:, other_b(at_ref, k, width)] for k in range(4)]
    else:
        width = og_ref.shape[1] // 2
        parts = [og_ref[:, half_a(at_ref, width)]] + [og_ref[:, block_b(at_ref, k, width)] for k in range(4)]
    rows = jnp.concatenate(parts, axis=1)
    for k, a_ref in enumerate((a0, a1, a2, a3)):
        s = block(at_ref[2], k, a_ref.shape[0])
        weight = jnp.concatenate([a_ref[...]] + [b[s, :] for b in (b0, b1, b2, b3)], axis=1)
        o_ref[:, s] = dot(rows, weight, 1, 1)


def grad_attn_body(mine_ref, theirs_ref, q_ref, g_ref, o_ref):
    g_ref[...] = (mine_ref[...] + theirs_ref[...]).astype(BF16)
    for h, s in head_slices():
        o_ref[h] = dot(q_ref[:, s], g_ref[:, s], 0, 0).astype(BF16)


def local(queries, keys, values, out_weight, out_grad):
    q, k, v, og = queries[0], keys[0], values[0], out_grad[0]
    tokens, inner = q.shape
    width = og.shape[1] // 2
    y, _, core, x, zh = [lax.axis_index(name) for name in AXES]
    at = jnp.stack([core, y, x, zh]).astype(jnp.int32)
    factor = (HEAD * tokens * 16) ** (-0.5)
    scale = (tokens * 16 * 16) ** (-0.5)
    rows = rows_spec(tokens)
    heads = (HEADS // PER,)
    token_flops = 2 * tokens * inner * HEAD

    oog = from_core(lax.dynamic_slice(og, (0, (1 - core) * width), (tokens, width)))

    key_states = call(
        states_body, shape((HEADS, HEAD, HEAD)), k, v,
        grid=heads, in_specs=[rows, rows], out_specs=STATE_SPEC, flops=token_flops, room=ALL_ROOM,
    )

    def exchange(states, reverse):
        by_head = lax.all_to_all(states, CTX, 0, 0)
        sums = call(functools.partial(scan_body, reverse), shape(by_head.shape), by_head, flops=by_head.size)
        return lax.all_to_all(sums, CTX, 0, 0)

    half, part = width // 2, width // 8
    wa = lax.dynamic_slice(out_weight, (0, core * width), (out_weight.shape[0], half))
    wb = lax.dynamic_slice(out_weight, (0, core * width + half + y * part), (out_weight.shape[0], part))
    wz = copies(jnp.concatenate([wa, wb], axis=1), "zh")
    z_rows = 4 * out_weight.shape[0]
    wa, wb = call(place_body, [shape((z_rows, half)), shape((z_rows, part))], at, *wz)
    xb = copies(wb, "x")
    xa = copies(wa, "x")
    wb = call(stack_body, shape((inner, part)), at, *xb)
    yb = copies(wb, "y")
    prior = exchange(key_states, False)

    attended = call(
        functools.partial(attended_body, factor), shape((inner, tokens)), q, k, v, prior,
        grid=heads, in_specs=[rows, rows, rows, STATE_SPEC],
        out_specs=pl.BlockSpec((PER * HEAD, tokens), lambda i: (i, 0)), flops=5 * token_flops,
    )
    partner = from_core(attended)

    gw_flops = 2 * inner * 2 * tokens * (width // 2)
    gy = call(
        weight_y_body, [shape((inner, width // 8))] * 4, at, attended, partner, og, oog,
        flops=gw_flops,
    )
    gx = call(
        weight_x_body, [shape((inner // 4, width // 2))] * 4, at, attended, partner, og, oog,
        flops=gw_flops,
    )
    project_flops = 2 * tokens * inner * width
    for_partner = call(
        functools.partial(projected_body, True), shape((tokens, inner), F32), at, oog, *xa, *yb,
        flops=project_flops,
    )
    from_partner = from_core(for_partner)

    mine = call(
        functools.partial(projected_body, False), shape((tokens, inner), F32), at, og, *xa, *yb,
        flops=project_flops,
    )
    gy = spread(gy, "y")
    gx = spread(gx, "x")
    ga, grad_states = call(
        grad_attn_body, [shape((tokens, inner)), shape((HEADS, HEAD, HEAD))], mine, from_partner, q,
        grid=heads, in_specs=[rows, rows, rows], out_specs=[rows, STATE_SPEC], flops=token_flops,
    )
    quarter = shape((inner // 4, width // 8))
    gyx = call(add_then_x_body, [quarter] * 4, at, *gy)
    gyx = spread(gyx, "x")
    later = exchange(grad_states, True)
    gxy = call(add_then_y_body, [quarter] * 4, at, *gx)
    gxy = spread(gxy, "y")
    grad_queries = call(
        functools.partial(grad_queries_body, factor), shape((tokens, inner)), ga, k, v, prior,
        grid=heads, in_specs=[rows, rows, rows, STATE_SPEC], out_specs=rows, flops=5 * token_flops, room=ALL_ROOM,
    )
    gz = call(add_then_z_body, shape((8, inner // 16, width // 8)), *gyx, *gxy)
    grad_keys, grad_values = call(
        functools.partial(grad_keys_values_body, factor), [shape((tokens, inner))] * 2, ga, q, k, v, later,
        grid=heads, in_specs=[rows, rows, rows, rows, STATE_SPEC], out_specs=[rows, rows], flops=10 * token_flops, room=ALL_ROOM,
    )
    gz = lax.all_to_all(gz, ("zl", "zh"), 0, 0)
    total = call(add_then_all_body, shape((16, inner // 16, width // 8)), gz)
    gathered = lax.all_to_all(total, CTX, 0, 0)
    grad_weight = call(functools.partial(finish_weight_body, scale), shape((inner // 16, 2 * width), F32), gathered)

    return grad_queries[None], grad_keys[None], grad_values[None], grad_weight


def solution(mesh):
    fine = jax.sharding.Mesh(mesh.devices.reshape(4, 2, 2, 4, 4), AXES)
    tokens, rows = P(FSDP, CTX, None), P(FSDP, None)

    return jax.shard_map(
        local, mesh=fine, in_specs=(tokens, tokens, tokens, rows, tokens), out_specs=(tokens, tokens, tokens, rows), check_vma=False
    )
```

```python
import functools
import math

import jax
import jax.numpy as jnp
from jax import lax
from jax.experimental import pallas as pl
from jax.experimental.pallas import tpu as pltpu
from jax.sharding import PartitionSpec as P

HEADS = 16
HEAD = 128
F32 = jnp.float32
BF16 = jnp.bfloat16

ALL_ROOM = 60 * 2**20


def dot(a, b, da, db):
    return lax.dot_general(a, b, (((da,), (db,)), ((), ())), preferred_element_type=F32)


AXES = ("y", "zl", "c", "x", "zh")
CTX, FSDP = AXES[:3], AXES[3:]


def from_core(v):
    return lax.ppermute(v, "c", [(0, 1), (1, 0)])


def copies(v, axis):
    return [v] + [lax.ppermute(v, axis, [((i + k) % 4, i) for i in range(4)]) for k in (1, 2, 3)]


def spread(pieces, axis):
    return [pieces[0]] + [
        lax.ppermute(pieces[k], axis, [(i, (i + k) % 4) for i in range(4)]) for k in (1, 2, 3)
    ]


def call(body, out, *args, grid=None, in_specs=None, out_specs=None, flops=0, room=None):
    size = sum(a.size * a.dtype.itemsize for a in args)
    outs = out if isinstance(out, (tuple, list)) else [out]
    size += sum(math.prod(o.shape) * jnp.dtype(o.dtype).itemsize for o in outs)
    kwargs = {}
    if grid is not None:
        kwargs = dict(grid=grid)
    else:
        full = pl.BlockSpec(memory_space=pltpu.VMEM)
        small = pl.BlockSpec(memory_space=pltpu.SMEM)
        in_specs = [small if a.dtype == jnp.int32 else full for a in args]
        out_specs = jax.tree.map(lambda o: full, out)
    if room is None:
        room = size + 6 * 2**20
    return pl.pallas_call(
        body,
        out_shape=out,
        in_specs=list(in_specs),
        out_specs=out_specs,
        cost_estimate=pl.CostEstimate(flops=flops, bytes_accessed=size, transcendentals=0),
        compiler_params=pltpu.CompilerParams(vmem_limit_bytes=room),
        **kwargs,
    )(*args)


def shape(dims, dtype=BF16):
    return jax.ShapeDtypeStruct(dims, dtype)


def in_hbm(dims, dtype=BF16):
    return pltpu.HBM(dims, dtype)


PER = 8


def head_slices():
    return [(h, slice(h * HEAD, (h + 1) * HEAD)) for h in range(PER)]


def rows_spec(tokens):
    return pl.BlockSpec((tokens, PER * HEAD), lambda i: (0, i))


STATE_SPEC = pl.BlockSpec((PER, HEAD, HEAD), lambda i: (i, 0, 0))


def states_body(a_ref, b_ref, o_ref):
    for h, s in head_slices():
        o_ref[h] = dot(a_ref[:, s], b_ref[:, s], 0, 0).astype(BF16)


def scan_body(reverse, i_ref, o_ref):
    count = i_ref.shape[0]
    total = jnp.zeros(i_ref.shape[1:], F32)
    for n in range(count):
        at = count - 1 - n if reverse else n
        o_ref[at] = total.astype(BF16)
        total = total + i_ref[at].astype(F32)


def causal(tokens):
    return lax.broadcasted_iota(jnp.int32, (tokens, tokens), 0) >= lax.broadcasted_iota(
        jnp.int32, (tokens, tokens), 1
    )


def attended_body(factor, q_ref, k_ref, v_ref, p_ref, o_ref):
    keep = causal(q_ref.shape[0])
    for h, s in head_slices():
        q = q_ref[:, s]
        scores = jnp.where(keep, dot(q, k_ref[:, s], 1, 1), 0.0).astype(BF16)
        o_ref[s, :] = (factor * (dot(p_ref[h], q, 0, 1) + dot(v_ref[:, s], scores, 0, 1))).astype(BF16)


def grad_queries_body(factor, g_ref, k_ref, v_ref, p_ref, o_ref):
    keep = causal(g_ref.shape[0])
    for h, s in head_slices():
        g = g_ref[:, s]
        reverse = jnp.where(keep, dot(g, v_ref[:, s], 1, 1), 0.0).astype(BF16)
        o_ref[:, s] = (factor * (dot(g, p_ref[h], 1, 1) + dot(reverse, k_ref[:, s], 1, 0))).astype(BF16)


def grad_keys_values_body(factor, g_ref, q_ref, k_ref, v_ref, l_ref, gk_ref, gv_ref):
    keep = causal(g_ref.shape[0])
    for h, s in head_slices():
        g, q, k, v, later = g_ref[:, s], q_ref[:, s], k_ref[:, s], v_ref[:, s], l_ref[h]
        scores = jnp.where(keep, dot(q, k, 1, 1), 0.0).astype(BF16)
        reverse = jnp.where(keep, dot(g, v, 1, 1), 0.0).astype(BF16)
        gk_ref[:, s] = (factor * (dot(v, later, 1, 1) + dot(reverse, q, 0, 0))).astype(BF16)
        gv_ref[:, s] = (factor * (dot(k, later, 1, 0) + dot(scores, g, 0, 0))).astype(BF16)


def block(at, k, size):
    return pl.ds(pl.multiple_of(lax.rem(at + k, 4) * size, size), size)


def half_a(at_ref, width):
    return pl.ds(pl.multiple_of(at_ref[0] * width, width), width // 2)


def block_b(at_ref, k, width):
    start = at_ref[0] * width + width // 2 + lax.rem(at_ref[1] + k, 4) * (width // 8)
    return pl.ds(pl.multiple_of(start, width // 8), width // 8)


def other_b(at_ref, k, width):
    start = width // 2 + lax.rem(at_ref[1] + k, 4) * (width // 8)
    return pl.ds(pl.multiple_of(start, width // 8), width // 8)


def weight_y_body(at_ref, mine_ref, theirs_ref, og_ref, oog_ref, *o_refs):
    width = oog_ref.shape[1]
    og = jnp.concatenate([og_ref[:, block_b(at_ref, k, width)] for k in range(4)], axis=1)
    oog = jnp.concatenate([oog_ref[:, other_b(at_ref, k, width)] for k in range(4)], axis=1)
    step = 512

    def body(r, carry):
        rows = pl.ds(pl.multiple_of(r * step, step), step)
        both = dot(mine_ref[rows, :], og, 1, 0) + dot(theirs_ref[rows, :], oog, 1, 0)
        for k in range(4):
            o_refs[k][rows, :] = both[:, k * (width // 8) : (k + 1) * (width // 8)].astype(BF16)
        return carry

    lax.fori_loop(0, mine_ref.shape[0] // step, body, 0)


def weight_x_body(at_ref, mine_ref, theirs_ref, og_ref, oog_ref, *o_refs):
    width = oog_ref.shape[1]
    og = og_ref[:, half_a(at_ref, width)]
    oog = oog_ref[:, : width // 2]
    step = 512
    size = o_refs[0].shape[0]
    for k in range(4):
        start = lax.rem(at_ref[2] + k, 4) * size

        def body(r, carry, start=start, k=k):
            rows = pl.ds(pl.multiple_of(start + r * step, step), step)
            both = dot(mine_ref[rows, :], og, 1, 0) + dot(theirs_ref[rows, :], oog, 1, 0)
            o_refs[k][pl.ds(pl.multiple_of(r * step, step), step), :] = both.astype(BF16)
            return carry

        lax.fori_loop(0, size // step, body, 0)


def added(refs):
    total = refs[0][...].astype(F32)
    for ref in refs[1:]:
        total = total + ref[...].astype(F32)
    return total


def add_then_x_body(at_ref, *refs):
    size = refs[0].shape[0] // 4
    for k in range(4):
        rows = block(at_ref[2], k, size)
        total = refs[0][rows, :].astype(F32)
        for ref in refs[1:4]:
            total = total + ref[rows, :].astype(F32)
        refs[4 + k][...] = total.astype(BF16)


def add_then_y_body(at_ref, *refs):
    size = refs[0].shape[1] // 4
    for k in range(4):
        columns = block(at_ref[1], k, size)
        total = refs[0][:, columns].astype(F32)
        for ref in refs[1:4]:
            total = total + ref[:, columns].astype(F32)
        refs[4 + k][...] = total.astype(BF16)


def add_then_z_body(*refs):
    size = refs[8].shape[1]
    for first, total in ((0, added(refs[:4])), (4, added(refs[4:8]))):
        for n in range(4):
            refs[8][first + n] = total[n * size : (n + 1) * size, :].astype(BF16)


def add_then_all_body(i_ref, o_ref):
    total = added([i_ref.at[n] for n in range(i_ref.shape[0])]).astype(BF16)
    for n in range(o_ref.shape[0]):
        o_ref[n] = total


def finish_weight_body(scale, i_ref, o_ref):
    for n in range(i_ref.shape[0]):
        y, zl, core = n // 4, n // 2 % 2, n % 2
        column = (core * 8 + (1 - zl) * 4 + y) * i_ref.shape[2]
        o_ref[:, column : column + i_ref.shape[2]] = i_ref[n].astype(F32) * scale


def place_body(at_ref, *refs):
    size = refs[0].shape[0]
    for k in range(4):
        refs[4][block(at_ref[3], k, size), :] = refs[k][...]


def stack_body(at_ref, *refs):
    size = refs[0].shape[0]
    for k in range(4):
        refs[4][block(at_ref[2], k, size), :] = refs[k][...]


def projected_body(other, at_ref, og_ref, a0, a1, a2, a3, b0, b1, b2, b3, o_ref):
    if other:
        width = og_ref.shape[1]
        parts = [og_ref[:, : width // 2]] + [og_ref[:, other_b(at_ref, k, width)] for k in range(4)]
    else:
        width = og_ref.shape[1] // 2
        parts = [og_ref[:, half_a(at_ref, width)]] + [og_ref[:, block_b(at_ref, k, width)] for k in range(4)]
    rows = jnp.concatenate(parts, axis=1)
    for k, a_ref in enumerate((a0, a1, a2, a3)):
        s = block(at_ref[2], k, a_ref.shape[0])
        weight = jnp.concatenate([a_ref[...]] + [b[s, :] for b in (b0, b1, b2, b3)], axis=1)
        o_ref[:, s] = dot(rows, weight, 1, 1)


def grad_attn_body(mine_ref, theirs_ref, q_ref, g_ref, o_ref):
    g_ref[...] = (mine_ref[...] + theirs_ref[...]).astype(BF16)
    for h, s in head_slices():
        o_ref[h] = dot(q_ref[:, s], g_ref[:, s], 0, 0).astype(BF16)


def local(queries, keys, values, out_weight, out_grad):
    q, k, v, og = queries[0], keys[0], values[0], out_grad[0]
    tokens, inner = q.shape
    width = og.shape[1] // 2
    y, _, core, x, zh = [lax.axis_index(name) for name in AXES]
    at = jnp.stack([core, y, x, zh]).astype(jnp.int32)
    factor = (HEAD * tokens * 16) ** (-0.5)
    scale = (tokens * 16 * 16) ** (-0.5)
    rows = rows_spec(tokens)
    heads = (HEADS // PER,)
    token_flops = 2 * tokens * inner * HEAD

    oog = from_core(lax.dynamic_slice(og, (0, (1 - core) * width), (tokens, width)))

    key_states = call(
        states_body, shape((HEADS, HEAD, HEAD)), k, v,
        grid=heads, in_specs=[rows, rows], out_specs=STATE_SPEC, flops=token_flops, room=ALL_ROOM,
    )

    def exchange(states, reverse):
        by_head = lax.all_to_all(states, CTX, 0, 0)
        sums = call(functools.partial(scan_body, reverse), in_hbm(by_head.shape), by_head, flops=by_head.size)
        return lax.all_to_all(sums, CTX, 0, 0)

    half, part = width // 2, width // 8
    wa = lax.dynamic_slice(out_weight, (0, core * width), (out_weight.shape[0], half))
    wb = lax.dynamic_slice(out_weight, (0, core * width + half + y * part), (out_weight.shape[0], part))
    zb = copies(wb, "zh")
    za = copies(wa, "zh")
    z_rows = 4 * out_weight.shape[0]
    wb = call(place_body, shape((z_rows, part)), at, *zb)
    wa = call(place_body, shape((z_rows, half)), at, *za)
    xb = copies(wb, "x")
    xa = copies(wa, "x")
    wb = call(stack_body, shape((inner, part)), at, *xb)
    yb = copies(wb, "y")
    prior = exchange(key_states, False)

    attended = call(
        functools.partial(attended_body, factor), shape((inner, tokens)), q, k, v, prior,
        grid=heads, in_specs=[rows, rows, rows, STATE_SPEC],
        out_specs=pl.BlockSpec((PER * HEAD, tokens), lambda i: (i, 0)), flops=5 * token_flops,
    )
    partner = from_core(attended)

    gw_flops = 2 * inner * 2 * tokens * (width // 2)
    gy = call(
        weight_y_body, [shape((inner, width // 8))] * 4, at, attended, partner, og, oog,
        flops=gw_flops,
    )
    gx = call(
        weight_x_body, [shape((inner // 4, width // 2))] * 4, at, attended, partner, og, oog,
        flops=gw_flops,
    )
    project_flops = 2 * tokens * inner * width
    for_partner = call(
        functools.partial(projected_body, True), shape((tokens, inner), F32), at, oog, *xa, *yb,
        flops=project_flops,
    )
    from_partner = from_core(for_partner)

    mine = call(
        functools.partial(projected_body, False), shape((tokens, inner), F32), at, og, *xa, *yb,
        flops=project_flops,
    )
    gy = spread(gy, "y")
    gx = spread(gx, "x")
    ga, grad_states = call(
        grad_attn_body, [in_hbm((tokens, inner)), in_hbm((HEADS, HEAD, HEAD))], mine, from_partner, q,
        grid=heads, in_specs=[rows, rows, rows], out_specs=[rows, STATE_SPEC], flops=token_flops,
    )
    quarter = shape((inner // 4, width // 8))
    gyx = call(add_then_x_body, [quarter] * 4, at, *gy)
    gyx = spread(gyx, "x")
    later = exchange(grad_states, True)
    gxy = call(add_then_y_body, [quarter] * 4, at, *gx)
    gxy = spread(gxy, "y")
    grad_queries = call(
        functools.partial(grad_queries_body, factor), shape((tokens, inner)), ga, k, v, prior,
        grid=heads, in_specs=[rows, rows, rows, STATE_SPEC], out_specs=rows, flops=5 * token_flops, room=ALL_ROOM,
    )
    gz = call(add_then_z_body, shape((8, inner // 16, width // 8)), *gyx, *gxy)
    grad_keys, grad_values = call(
        functools.partial(grad_keys_values_body, factor), [shape((tokens, inner))] * 2, ga, q, k, v, later,
        grid=heads, in_specs=[rows, rows, rows, rows, STATE_SPEC], out_specs=[rows, rows], flops=10 * token_flops, room=ALL_ROOM,
    )
    gz = lax.all_to_all(gz, ("zl", "zh"), 0, 0)
    total = call(add_then_all_body, in_hbm((16, inner // 16, width // 8)), gz)
    gathered = lax.all_to_all(total, CTX, 0, 0)
    grad_weight = call(functools.partial(finish_weight_body, scale), shape((inner // 16, 2 * width), F32), gathered)

    return grad_queries[None], grad_keys[None], grad_values[None], grad_weight


def solution(mesh):
    fine = jax.sharding.Mesh(mesh.devices.reshape(4, 2, 2, 4, 4), AXES)
    tokens, rows = P(FSDP, CTX, None), P(FSDP, None)

    return jax.shard_map(
        local, mesh=fine, in_specs=(tokens, tokens, tokens, rows, tokens), out_specs=(tokens, tokens, tokens, rows), check_vma=False
    )
```

```python
import functools
import math

import jax
import jax.numpy as jnp
from jax import lax
from jax.experimental import pallas as pl
from jax.experimental.pallas import tpu as pltpu
from jax.sharding import PartitionSpec as P

HEADS = 16
HEAD = 128
F32 = jnp.float32
BF16 = jnp.bfloat16

ALL_ROOM = 60 * 2**20


def dot(a, b, da, db):
    return lax.dot_general(a, b, (((da,), (db,)), ((), ())), preferred_element_type=F32)


AXES = ("y", "zl", "c", "x", "zh")
CTX, FSDP = AXES[:3], AXES[3:]


def from_core(v):
    return lax.ppermute(v, "c", [(0, 1), (1, 0)])


def copies(v, axis):
    return [v] + [lax.ppermute(v, axis, [((i + k) % 4, i) for i in range(4)]) for k in (1, 2, 3)]


def spread(pieces, axis):
    return [pieces[0]] + [
        lax.ppermute(pieces[k], axis, [(i, (i + k) % 4) for i in range(4)]) for k in (1, 2, 3)
    ]


def call(body, out, *args, grid=None, in_specs=None, out_specs=None, flops=0, room=None):
    size = sum(a.size * a.dtype.itemsize for a in args)
    outs = out if isinstance(out, (tuple, list)) else [out]
    size += sum(math.prod(o.shape) * jnp.dtype(o.dtype).itemsize for o in outs)
    kwargs = {}
    if grid is not None:
        kwargs = dict(grid=grid)
    else:
        full = pl.BlockSpec(memory_space=pltpu.VMEM)
        small = pl.BlockSpec(memory_space=pltpu.SMEM)
        in_specs = [small if a.dtype == jnp.int32 else full for a in args]
        out_specs = jax.tree.map(lambda o: full, out)
    if room is None:
        room = size + 6 * 2**20
    return pl.pallas_call(
        body,
        out_shape=out,
        in_specs=list(in_specs),
        out_specs=out_specs,
        cost_estimate=pl.CostEstimate(flops=flops, bytes_accessed=size, transcendentals=0),
        compiler_params=pltpu.CompilerParams(vmem_limit_bytes=room),
        **kwargs,
    )(*args)


def shape(dims, dtype=BF16):
    return jax.ShapeDtypeStruct(dims, dtype)


def in_hbm(dims, dtype=BF16):
    return pltpu.HBM(dims, dtype)


PER = 8


def head_slices(ref):
    return [(h, slice(h * HEAD, (h + 1) * HEAD)) for h in range(ref.shape[1] // HEAD)]


def rows_spec(tokens, per=PER):
    return pl.BlockSpec((tokens, per * HEAD), lambda i: (0, i))


def state_spec(per=PER):
    return pl.BlockSpec((per, HEAD, HEAD), lambda i: (i, 0, 0))


STATE_SPEC = state_spec()


def states_body(a_ref, b_ref, o_ref):
    for h, s in head_slices(a_ref):
        o_ref[h] = dot(a_ref[:, s], b_ref[:, s], 0, 0).astype(BF16)


def key_states_body(at_ref, a_ref, b_ref, g_ref, o_ref, h_ref):
    states_body(a_ref, b_ref, o_ref)
    h_ref[...] = g_ref[...]


def scan_body(reverse, i_ref, o_ref):
    count = i_ref.shape[0]
    total = jnp.zeros(i_ref.shape[1:], F32)
    for n in range(count):
        at = count - 1 - n if reverse else n
        o_ref[at] = total.astype(BF16)
        total = total + i_ref[at].astype(F32)


def causal(tokens):
    return lax.broadcasted_iota(jnp.int32, (tokens, tokens), 0) >= lax.broadcasted_iota(
        jnp.int32, (tokens, tokens), 1
    )


def attended_body(factor, q_ref, k_ref, v_ref, p_ref, o_ref):
    keep = causal(q_ref.shape[0])
    for h, s in head_slices(q_ref):
        q = q_ref[:, s]
        scores = jnp.where(keep, dot(q, k_ref[:, s], 1, 1), 0.0).astype(BF16)
        o_ref[s, :] = (factor * (dot(p_ref[h], q, 0, 1) + dot(v_ref[:, s], scores, 0, 1))).astype(BF16)


def grad_queries_body(factor, g_ref, k_ref, v_ref, p_ref, o_ref):
    keep = causal(g_ref.shape[0])
    for h, s in head_slices(g_ref):
        g = g_ref[:, s]
        reverse = jnp.where(keep, dot(g, v_ref[:, s], 1, 1), 0.0).astype(BF16)
        o_ref[:, s] = (factor * (dot(g, p_ref[h], 1, 1) + dot(reverse, k_ref[:, s], 1, 0))).astype(BF16)


def grad_keys_values_body(factor, g_ref, q_ref, k_ref, v_ref, l_ref, gk_ref, gv_ref):
    keep = causal(g_ref.shape[0])
    for h, s in head_slices(g_ref):
        g, q, k, v, later = g_ref[:, s], q_ref[:, s], k_ref[:, s], v_ref[:, s], l_ref[h]
        scores = jnp.where(keep, dot(q, k, 1, 1), 0.0).astype(BF16)
        reverse = jnp.where(keep, dot(g, v, 1, 1), 0.0).astype(BF16)
        gk_ref[:, s] = (factor * (dot(v, later, 1, 1) + dot(reverse, q, 0, 0))).astype(BF16)
        gv_ref[:, s] = (factor * (dot(k, later, 1, 0) + dot(scores, g, 0, 0))).astype(BF16)


def block(at, k, size):
    return pl.ds(pl.multiple_of(lax.rem(at + k, 4) * size, size), size)


def half_a(at_ref, width):
    return pl.ds(pl.multiple_of(at_ref[0] * width, width), width // 2)


def block_b(at_ref, k, width):
    start = at_ref[0] * width + width // 2 + lax.rem(at_ref[1] + k, 4) * (width // 8)
    return pl.ds(pl.multiple_of(start, width // 8), width // 8)


def other_b(at_ref, k, width):
    start = width // 2 + lax.rem(at_ref[1] + k, 4) * (width // 8)
    return pl.ds(pl.multiple_of(start, width // 8), width // 8)


def weight_y_body(at_ref, mine_ref, theirs_ref, og_ref, oog_ref, *o_refs):
    width = oog_ref.shape[1]
    part = width // 8
    og = jnp.concatenate(
        [
            jnp.concatenate([og_ref[:, block_b(at_ref, k, width)] for k in range(4)], axis=1),
            jnp.concatenate([oog_ref[:, other_b(at_ref, k, width)] for k in range(4)], axis=1),
        ],
        axis=0,
    )
    step = 512
    for r in range(0, mine_ref.shape[0], step):
        rows = slice(r, r + step)
        both = dot(jnp.concatenate([mine_ref[rows, :], theirs_ref[rows, :]], axis=1), og, 1, 0).astype(BF16)
        for k in range(4):
            o_refs[k][rows, :] = both[:, k * part : (k + 1) * part]


def weight_x_body(at_ref, mine_ref, theirs_ref, og_ref, oog_ref, *o_refs):
    width = oog_ref.shape[1]
    og = jnp.concatenate([og_ref[:, half_a(at_ref, width)], oog_ref[:, : width // 2]], axis=0)
    for k in range(4):
        rows = block(at_ref[2], k, o_refs[k].shape[0])
        o_refs[k][...] = dot(jnp.concatenate([mine_ref[rows, :], theirs_ref[rows, :]], axis=1), og, 1, 0).astype(BF16)


def added(refs):
    total = refs[0][...].astype(F32)
    for ref in refs[1:]:
        total = total + ref[...].astype(F32)
    return total


def add_then_x_body(at_ref, *refs):
    size = refs[0].shape[0] // 4
    for k in range(4):
        rows = block(at_ref[2], k, size)
        total = refs[0][rows, :].astype(F32)
        for ref in refs[1:4]:
            total = total + ref[rows, :].astype(F32)
        refs[4 + k][...] = total.astype(BF16)


def add_then_y_body(at_ref, *refs):
    size = refs[0].shape[1] // 4
    for k in range(4):
        columns = block(at_ref[1], k, size)
        total = refs[0][:, columns].astype(F32)
        for ref in refs[1:4]:
            total = total + ref[:, columns].astype(F32)
        refs[4 + k][...] = total.astype(BF16)


def add_then_z_body(at_ref, *refs):
    size = refs[8].shape[0]
    low = at_ref[4] == 0
    for k in range(4):
        s = block(at_ref[3], k, size)
        via_x, via_y = added([ref.at[s, :] for ref in refs[:4]]), added([ref.at[s, :] for ref in refs[4:8]])
        refs[8 + k][...] = jnp.where(low, via_x, via_y).astype(BF16)
        refs[12 + k][...] = jnp.where(low, via_y, via_x).astype(BF16)


def add_then_all_body(*refs):
    total = added(refs[:8]).astype(BF16)
    for n in range(refs[8].shape[0]):
        refs[8][n] = total


def finish_weight_body(scale, i_ref, o_ref):
    for n in range(i_ref.shape[0]):
        y, zl, core = n // 4, n // 2 % 2, n % 2
        column = (core * 8 + (1 - zl) * 4 + y) * i_ref.shape[2]
        o_ref[:, column : column + i_ref.shape[2]] = i_ref[n].astype(F32) * scale


def place_body(at_ref, *refs):
    size = refs[0].shape[0]
    for k in range(4):
        refs[4][block(at_ref[3], k, size), :] = refs[k][...]


def stack_body(at_ref, *refs):
    size = refs[0].shape[0]
    for k in range(4):
        refs[4][block(at_ref[2], k, size), :] = refs[k][...]


def projected_body(other, at_ref, og_ref, a0, a1, c0, c1, c2, c3, o_ref):
    split = a0.shape[1]
    base = 0 if other else at_ref[0] * (4 * split)
    parts = [
        og_ref[:, pl.ds(pl.multiple_of(base + lax.rem(at_ref[4] + n, 2) * split, split), split)] for n in range(2)
    ]
    parts.append(og_ref[:, pl.ds(pl.multiple_of(base + 2 * split, 2 * split), 2 * split)])
    rows = jnp.concatenate(parts, axis=1)
    for k, c_ref in enumerate((c0, c1, c2, c3)):
        s = block(at_ref[2], k, c_ref.shape[0])
        weight = jnp.concatenate([a0[s, :], a1[s, :], c_ref[...]], axis=1)
        o_ref[:, s] = dot(rows, weight, 1, 1)


def grad_attn_body(mine_ref, theirs_ref, q_ref, g_ref, o_ref):
    g_ref[...] = (mine_ref[...] + theirs_ref[...]).astype(BF16)
    for h, s in head_slices(mine_ref):
        o_ref[h] = dot(q_ref[:, s], g_ref[:, s], 0, 0).astype(BF16)


def local(queries, keys, values, out_weight, out_grad):
    q, k, v, og = queries[0], keys[0], values[0], out_grad[0]
    tokens, inner = q.shape
    width = og.shape[1] // 2
    y, zl, core, x, zh = [lax.axis_index(name) for name in AXES]
    at = jnp.stack([core, y, x, zh, zl]).astype(jnp.int32)
    factor = (HEAD * tokens * 16) ** (-0.5)
    scale = (tokens * 16 * 16) ** (-0.5)
    rows = rows_spec(tokens)
    heads = (HEADS // PER,)
    token_flops = 2 * tokens * inner * HEAD

    steps = HEADS // PER
    half_rows = pl.BlockSpec((tokens // steps, width), lambda i, at_ref: (i, 1 - at_ref[0]))
    rows_at = pl.BlockSpec((tokens, PER * HEAD), lambda i, at_ref: (0, i))
    key_states, half_og = pl.pallas_call(
        key_states_body,
        out_shape=[in_hbm((HEADS, HEAD, HEAD)), in_hbm((tokens, width))],
        grid_spec=pltpu.PrefetchScalarGridSpec(
            num_scalar_prefetch=1,
            grid=heads,
            in_specs=[rows_at, rows_at, half_rows],
            out_specs=[
                pl.BlockSpec((PER, HEAD, HEAD), lambda i, at_ref: (i, 0, 0)),
                pl.BlockSpec((tokens // steps, width), lambda i, at_ref: (i, 0)),
            ],
        ),
        cost_estimate=pl.CostEstimate(flops=token_flops, bytes_accessed=3 * k.size * 2, transcendentals=0),
        compiler_params=pltpu.CompilerParams(vmem_limit_bytes=ALL_ROOM),
        name="key_states",
    )(at, k, v, og)
    oog = from_core(half_og)

    def exchange(states, reverse):
        by_head = lax.all_to_all(states, CTX, 0, 0)
        sums = call(functools.partial(scan_body, reverse), in_hbm(by_head.shape), by_head, flops=by_head.size)
        return lax.all_to_all(sums, CTX, 0, 0)

    half = width // 2
    quarter_cols = half // 2
    wa = lax.dynamic_slice(out_weight, (0, core * width + zl * quarter_cols), (out_weight.shape[0], quarter_cols))
    wc = lax.dynamic_slice(out_weight, (0, core * width + half), (out_weight.shape[0], half))
    za = copies(wa, "zh")
    zc = copies(wc, "zh")
    z_rows = 4 * out_weight.shape[0]
    wa = call(place_body, shape((z_rows, quarter_cols)), at, *za)
    wc = call(place_body, shape((z_rows, half)), at, *zc)
    xa = copies(wa, "x")
    xc = copies(wc, "x")
    wa = call(stack_body, shape((inner, quarter_cols)), at, *xa)
    za = [wa, lax.ppermute(wa, "zl", [(0, 1), (1, 0)])]
    prior = exchange(key_states, False)

    attended = call(
        functools.partial(attended_body, factor), shape((inner, tokens)), q, k, v, prior,
        grid=heads, in_specs=[rows, rows, rows, STATE_SPEC],
        out_specs=pl.BlockSpec((PER * HEAD, tokens), lambda i: (i, 0)), flops=5 * token_flops,
    )
    partner = from_core(attended)

    gw_flops = 2 * inner * 2 * tokens * (width // 2)
    gy = call(
        weight_y_body, [shape((inner, width // 8))] * 4, at, attended, partner, og, oog,
        flops=gw_flops,
    )
    gx = call(
        weight_x_body, [shape((inner // 4, width // 2))] * 4, at, attended, partner, og, oog,
        flops=gw_flops,
    )
    project_flops = 2 * tokens * inner * width
    for_partner = call(
        functools.partial(projected_body, True), shape((tokens, inner), F32), at, oog, *za, *xc,
        flops=project_flops,
    )
    from_partner = from_core(for_partner)

    mine = call(
        functools.partial(projected_body, False), shape((tokens, inner), F32), at, og, *za, *xc,
        flops=project_flops,
    )
    gy = spread(gy, "y")
    gx = spread(gx, "x")
    ga, grad_states = call(
        grad_attn_body, [in_hbm((tokens, inner)), in_hbm((HEADS, HEAD, HEAD))], mine, from_partner, q,
        grid=heads, in_specs=[rows, rows, rows], out_specs=[rows, STATE_SPEC], flops=token_flops,
    )
    quarter = shape((inner // 4, width // 8))
    gyx = call(add_then_x_body, [quarter] * 4, at, *gy)
    gyx = spread(gyx, "x")
    later = exchange(grad_states, True)
    gxy = call(add_then_y_body, [quarter] * 4, at, *gx)
    gxy = spread(gxy, "y")
    few, small, small_state = (HEADS // 4,), rows_spec(tokens, 4), state_spec(4)
    grad_queries = call(
        functools.partial(grad_queries_body, factor), shape((tokens, inner)), ga, k, v, prior,
        grid=heads, in_specs=[rows, rows, rows, STATE_SPEC], out_specs=rows, flops=5 * token_flops, room=ALL_ROOM,
    )
    gz = call(add_then_z_body, [shape((inner // 16, width // 8))] * 8, at, *gyx, *gxy)
    grad_keys, grad_values = call(
        functools.partial(grad_keys_values_body, factor), [shape((tokens, inner))] * 2, ga, q, k, v, later,
        grid=few, in_specs=[small, small, small, small, small_state], out_specs=[small, small], flops=10 * token_flops, room=ALL_ROOM,
    )
    gz = [gz[0]] + [
        lax.ppermute(gz[n], ("zl", "zh"), [(i, (i // 4 ^ n // 4) * 4 + (i + n) % 4) for i in range(8)])
        for n in (4, 1, 3, 5, 7, 2, 6)
    ]
    total = call(add_then_all_body, in_hbm((16, inner // 16, width // 8)), *gz)
    gathered = lax.all_to_all(total, CTX, 0, 0)
    grad_weight = call(functools.partial(finish_weight_body, scale), shape((inner // 16, 2 * width), F32), gathered)

    return grad_queries[None], grad_keys[None], grad_values[None], grad_weight


def solution(mesh):
    fine = jax.sharding.Mesh(mesh.devices.reshape(4, 2, 2, 4, 4), AXES)
    tokens, rows = P(FSDP, CTX, None), P(FSDP, None)

    return jax.shard_map(
        local, mesh=fine, in_specs=(tokens, tokens, tokens, rows, tokens), out_specs=(tokens, tokens, tokens, rows), check_vma=False
    )
```
